32 devices in a mesh: dp: 2 (over core), space: 4 (over y, x), heads: 4 (over z).
Axes of the slice: x: 2, y: 2, z: 4, core: 2. Of those that a mesh axis runs over, the one named last changes fastest.
Arguments:
- queries: bfloat16 [8192, 5120], P(('dp', 'space'), 'heads'), parts along dimension 0
- keys: bfloat16 [8192, 5120], P(('dp', 'space'), 'heads'), parts along dimension 0
- values: bfloat16 [8192, 5120], P(('dp', 'space'), 'heads'), parts along dimension 0, may hold values from -6 to 6
- cache_keys: bfloat16 [256, 16, 5120], P(('dp', 'space', 'heads')), parts along dimension 0, may hold values from -15 to 15
- cache_values: bfloat16 [256, 16, 5120], P(('dp', 'space', 'heads')), parts along dimension 0, may hold values from -6 to 6
- block_list: int32 [8, 24], P('dp'), parts along dimension 0, may hold values from 0 to 127, as said below
- block_counts: int32 [8], P('dp'), parts along dimension 0, may hold values from 12 to 24, as said below
Outputs:
- attended: bfloat16 [8192, 5120], P(('dp', 'space'), 'heads'), parts along dimension 0
The draws below stay inside these ranges and needn't reach their ends.
There are 2 independent parts, one for each index of `dp`. The reference program is written for one: setup_inputs(seed, part) draws one part's arguments, and reference() takes and returns one part's arrays. A program takes and returns all parts, laid end to end along the dimension named above; each array names one. Nothing has to cross between parts.
Inputs may be any that keep to these rules, and one draw needn't show every extreme that they name: `block_list`: each list names 24 different blocks in some order; block b is held by device b // 8 of the joined space and heads axes; a list names exactly 2 blocks of every device it names and none of the others. `block_counts`: some tile reads its whole list.
All inputs are finite; a program needn't handle non-finite values.
Results may differ from the reference program's by a relative error of at most 0.005.
Values may be sent and summed in bfloat16 or wider, within the bound.
A program may use at most 128 MiB of HBM per device.

```python
import jax
import jax.numpy as jnp
from jax import lax

HEADS = 40
HS = 128
TOK_DEV = 1024
BLK = 16
BPD = 8
CAP = 2
TILES = 4
OWNERS = 16
BLOCKS = 128
LIST = 24
TOKENS = 4096


def shared_rows(key):
    base_key = jax.random.fold_in(key, 101)
    key_a, key_b = jax.random.split(base_key, 2)
    draw_shape = (TOKENS, HEADS * HS)
    query_draw = jnp.clip(jax.random.normal(key_a, draw_shape, jnp.float32), -6.0, 6.0)
    key_draw = jnp.clip(2.5 * jax.random.normal(key_b, draw_shape, jnp.float32), -15.0, 15.0)
    return (query_draw, key_draw)


def draw_queries(key, part):
    return shared_rows(key)[0].astype(jnp.bfloat16)


def draw_keys(key, part):
    return shared_rows(key)[1].astype(jnp.bfloat16)


def draw_block_list(key, part):
    owner_picks = LIST // CAP

    def one_row(row_key):
        key_a, key_b, key_c = jax.random.split(row_key, 3)
        chosen = jax.random.permutation(key_a, OWNERS)[:owner_picks]
        first_local = jax.random.randint(key_b, (owner_picks,), 0, BPD)
        local_ids = (first_local[:, None] + jnp.arange(CAP)[None, :]) % BPD
        block_ids = (chosen[:, None] * BPD + local_ids).reshape(-1)
        return jax.random.permutation(key_c, block_ids)
    row_keys = jax.random.split(jax.random.fold_in(key, 7), TILES)
    return jax.vmap(one_row)(row_keys).astype(jnp.int32)


def draw_block_counts(key, part):
    key_a, key_b = jax.random.split(jax.random.fold_in(key, 13))
    counts = jax.random.randint(key_a, (TILES,), LIST // 2, LIST + 1)
    full_tile = jax.random.randint(key_b, (), 0, TILES)
    return jnp.where(jnp.arange(TILES) == full_tile, LIST, counts).astype(jnp.int32)


def shard_levels(key, extent, pieces, smallest, largest):
    def one(axis_at, shards_of):
        steps = jax.random.uniform(jax.random.fold_in(jax.random.fold_in(key, 6), axis_at), (shards_of,), jnp.float32, smallest / len(pieces), largest / len(pieces))
        return jnp.repeat(jnp.exp(steps), extent[axis_at] // shards_of).reshape((-1,) + (1,) * (len(extent) - axis_at - 1))

    loudness = one(*pieces[0])
    for cut in pieces[1:]:
        loudness = loudness * one(*cut)
    return loudness


def bell_draw(key, dims, scale, most, pieces=(), kind=jnp.bfloat16):
    values = scale * jax.random.normal(key, dims, jnp.float32)
    if pieces:
        values = values * shard_levels(key, dims, pieces, -0.22, 0.18)
    return jnp.clip(values, -most, most).astype(kind)


def setup_inputs(seed: int = 0, part: int = 0) -> dict:
    splits = jax.random.split(jax.random.key(seed), 8)
    own_keys = jax.random.split(jax.random.fold_in(splits[7], part), 8)
    queries = draw_queries(jax.random.fold_in(jax.random.fold_in(splits[7], part), 71), part)
    keys = draw_keys(jax.random.fold_in(jax.random.fold_in(splits[7], part), 71), part)
    values = bell_draw(own_keys[2], (TOKENS, HEADS * HS), 1.0, 6.0, ((0, 4), (1, 4)))
    cache_keys = bell_draw(own_keys[3], (BLOCKS, BLK, HEADS * HS), 2.5, 15.0, ((0, 16),))
    cache_values = bell_draw(own_keys[4], (BLOCKS, BLK, HEADS * HS), 1.0, 6.0, ((0, 16),))
    block_list = draw_block_list(jax.random.fold_in(jax.random.fold_in(splits[7], part), 71), part)
    block_counts = draw_block_counts(jax.random.fold_in(jax.random.fold_in(splits[7], part), 71), part)
    return {"queries": queries, "keys": keys, "values": values, "cache_keys": cache_keys, "cache_values": cache_values, "block_list": block_list, "block_counts": block_counts}


NEG_FILL = -1.0e30


def softmax_rows(query_rows, key_head, value_head, key_valid):
    scores = jnp.einsum("qd,kd->qk", query_rows, key_head, preferred_element_type=jnp.float32) * (HS ** -0.5)
    scores = jnp.where(key_valid[None, :], scores, NEG_FILL)
    row_top = jnp.max(scores, axis=1, keepdims=True)
    row_exp = jnp.where(key_valid[None, :], jnp.exp(scores - row_top), 0.0)
    weights = (row_exp / jnp.sum(row_exp, axis=1, keepdims=True)).astype(jnp.bfloat16)
    return jnp.dot(weights, value_head, preferred_element_type=jnp.float32).astype(jnp.bfloat16)


def attend(query_local, key_all, value_all, key_valid):
    tok_rows, col_width = query_local.shape
    heads_here = col_width // HS
    block_len = 512 if tok_rows % 512 == 0 else tok_rows
    query_heads = query_local.reshape(tok_rows // block_len, block_len, heads_here, HS).transpose(2, 0, 1, 3)
    key_heads = key_all.reshape(-1, heads_here, HS).transpose(1, 0, 2)
    value_heads = value_all.reshape(-1, heads_here, HS).transpose(1, 0, 2)

    def one_head(operands):
        query_blocks, key_head, value_head = operands

        def one_block(query_rows):
            return softmax_rows(query_rows, key_head, value_head, key_valid)

        return lax.map(one_block, query_blocks)

    result = lax.map(one_head, (query_heads, key_heads, value_heads))
    return result.transpose(1, 2, 0, 3).reshape(tok_rows, col_width)


def reference(queries, keys, values, cache_keys, cache_values, block_list, block_counts):
    keys_padded = jnp.pad(keys, ((TOK_DEV, TOK_DEV), (0, 0)))
    values_padded = jnp.pad(values, ((TOK_DEV, TOK_DEV), (0, 0)))

    def one_tile(tile_index):
        start = (tile_index * TOK_DEV).astype(jnp.int32)
        query_tile = lax.dynamic_slice_in_dim(queries, start, TOK_DEV, 0)
        key_window = lax.dynamic_slice_in_dim(keys_padded, start, 3 * TOK_DEV, 0)
        value_window = lax.dynamic_slice_in_dim(values_padded, start, 3 * TOK_DEV, 0)
        tile_of_key = jnp.arange(3 * TOK_DEV, dtype=jnp.int32) // TOK_DEV - 1 + tile_index
        window_valid = (tile_of_key >= 0) & (tile_of_key < TILES)
        block_ids = block_list[tile_index]
        key_cached = jnp.take(cache_keys, block_ids, axis=0).reshape(LIST * BLK, HEADS * HS)
        value_cached = jnp.take(cache_values, block_ids, axis=0).reshape(LIST * BLK, HEADS * HS)
        cached_valid = jnp.repeat(jnp.arange(LIST, dtype=jnp.int32) < block_counts[tile_index], BLK)
        key_all = jnp.concatenate((key_window, key_cached), axis=0)
        value_all = jnp.concatenate((value_window, value_cached), axis=0)
        key_valid = jnp.concatenate((window_valid, cached_valid), axis=0)
        return attend(query_tile, key_all, value_all, key_valid)

    result = lax.map(one_tile, jnp.arange(TILES, dtype=jnp.int32))
    return result.reshape(TOKENS, HEADS * HS)
```

```python
import functools

import jax
import jax.numpy as jnp
from jax import lax
from jax.experimental import pallas as pl
from jax.experimental.pallas import tpu as pltpu
from jax.sharding import PartitionSpec as P

HS = 128
CAP = 2
Q_ROWS = 256
LAG = 4
EXP_SCALE = HS ** (-0.5) * 1.4426950408889634
MESH = pl.DeviceIdType.MESH


def side_kernel(
    groups, waves, list_ref, count_ref, q_hbm, k_ref, v_ref, cache_k, cache_v, o_hbm,
    q_own, own, q_near, q_far, cache, out_blocks, arrived,
    own_part, own_log, sent_part, sent_log, got_part, got_log, far_part, far_log, result,
    q_send, q_recv, relay_send, relay_recv, part_send, part_recv, far_send, far_recv,
    block_send, block_recv, q_sem, own_sem, cache_sem, result_sem,
):
    tok_rows, col_width = k_ref.shape
    per_owner, block_rows, _ = cache_k.shape
    listed = list_ref.shape[1]
    heads_here = col_width // HS
    wave_heads = heads_here // waves
    side = 2 * groups
    video = lax.axis_index("dp")
    tile = lax.axis_index("space")
    group = lax.axis_index("heads")
    odd = lax.rem(tile, 2)
    tile_y = tile // 2
    near_tile = tile + 1 - 2 * odd
    far_tile = lax.rem(tile + 2, 4)
    me = tile_y * groups + group
    is_end = jnp.logical_or(tile == 0, tile == 3)
    is_mid = jnp.logical_not(is_end)
    near_device = (video, near_tile, group)
    far_device = (video, far_tile, group)

    def columns(h):
        return pl.ds(pl.multiple_of(h * HS, HS), HS)

    def cache_load(which):
        return pltpu.make_async_copy(
            (cache_k, cache_v)[which], cache.at[which], cache_sem.at[which]
        )

    def query_load(h):
        return pltpu.make_async_copy(q_hbm.at[:, columns(h)], q_own.at[h], q_sem.at[h])

    def own_load(h, which):
        return pltpu.make_async_copy(
            (k_ref, v_ref)[which].at[:, columns(h)], own.at[which, h], own_sem.at[which, h]
        )

    def result_store(h):
        return pltpu.make_async_copy(result.at[h], o_hbm.at[:, columns(h)], result_sem.at[h])

    def remote(src, dst, send_sem, recv_sem, device):
        return pltpu.make_async_remote_copy(
            src_ref=src, dst_ref=dst, send_sem=send_sem, recv_sem=recv_sem,
            device_id=device, device_id_type=MESH,
        )

    def query_copy(h):
        return remote(
            q_hbm.at[:, columns(h)], q_near.at[h], q_send.at[h], q_recv.at[h], near_device
        )

    def relay_copy(h):
        return remote(q_near.at[h], q_far.at[h], relay_send.at[h], relay_recv.at[h], far_device)

    def part_copy(h, which):
        src, dst = ((sent_part, got_part), (sent_log, got_log))[which]
        return remote(
            src.at[h], dst.at[h], part_send.at[which, h], part_recv.at[which, h], near_device
        )

    def far_copy(h, which):
        buffer = (far_part, far_log)[which]
        return remote(
            buffer.at[h], buffer.at[h], far_send.at[which, h], far_recv.at[which, h], far_device
        )

    def peer(offset):
        other = lax.rem(me + offset, side)
        return other, (video, odd + 2 * (other // groups), lax.rem(other, groups))

    def wave_part(wave):
        return pl.ds(wave * wave_heads, wave_heads)

    def block_copy(wave, offset):
        other, device = peer(offset)
        return remote(
            out_blocks.at[wave_part(wave), other], arrived.at[wave_part(wave), me],
            block_send.at[wave, offset], block_recv.at[wave, me], device,
        )

    def block_arrival(wave, offset):
        other, device = peer(offset)
        return remote(
            out_blocks.at[wave_part(wave), other], arrived.at[wave_part(wave), other],
            block_send.at[wave, offset], block_recv.at[wave, other], device,
        )

    def start_loads(h, carry):
        query_load(h).start()
        for which in range(2):
            own_load(h, which).start()
        return carry

    for which in range(2):
        cache_load(which).start()

    barrier = pltpu.get_barrier_semaphore()

    def announce(offset, carry):
        _, device = peer(offset)
        pl.semaphore_signal(barrier, inc=1, device_id=device, device_id_type=MESH)
        return carry

    pl.semaphore_signal(barrier, inc=1, device_id=near_device, device_id_type=MESH)
    lax.fori_loop(1, side, announce, 0)
    lax.fori_loop(0, heads_here, start_loads, 0)
    pl.semaphore_wait(barrier, side)

    def start_queries(h, carry):
        query_copy(h).start()
        return carry

    lax.fori_loop(0, heads_here, start_queries, 0)
    for which in range(2):
        cache_load(which).wait()

    def pack(to_tile, carry):
        def pick(m, state):
            seen, *ids = state
            block = list_ref[to_tile, m]
            owner = block // per_owner
            mine = jnp.logical_and(owner == tile * groups + group, m < count_ref[to_tile])
            ids = [
                jnp.where(jnp.logical_and(mine, seen == slot), lax.rem(block, per_owner), ids[slot])
                for slot in range(CAP)
            ]
            return (seen + mine.astype(jnp.int32), *ids)

        zero = jnp.int32(0)
        _, *ids = lax.fori_loop(0, listed, pick, (zero,) * (CAP + 1))
        crossed = lax.rem(to_tile + odd, 2)
        for which in range(2):
            for slot in range(CAP):
                block = cache[which, ids[slot]]
                for to_group in range(groups):
                    for h in range(heads_here):
                        start = to_group * col_width + h * HS
                        out_blocks[
                            h, to_tile // 2 * groups + to_group, crossed, which,
                            pl.ds(slot * block_rows, block_rows), :
                        ] = block[:, start : start + HS]
        return carry

    lax.fori_loop(0, 4, pack, 0)

    def start_blocks(wave):
        def start(offset, carry):
            block_copy(wave, offset).start()
            return carry

        lax.fori_loop(1, side, start, 0)

    for wave in range(waves):
        start_blocks(wave)

    slots_wide = side * CAP * block_rows
    lane = lax.broadcasted_iota(jnp.int32, (1, slots_wide), 1)
    lane_side = lane // (CAP * block_rows)
    lane_owner = (odd + 2 * (lane_side // groups)) * groups + lax.rem(lane_side, groups)
    lane_slot = lax.rem(lane // block_rows, CAP)

    def bias_of(list_tile):
        def hold(m, held):
            live = m < count_ref[list_tile]
            owner = jnp.where(live, list_ref[list_tile, m] // per_owner, -1)
            return held + (lane_owner == owner).astype(jnp.int32)

        held = lax.fori_loop(0, listed, hold, jnp.zeros((1, slots_wide), jnp.int32))
        return jnp.where(lane_slot < held, 0.0, -jnp.inf).astype(jnp.float32)

    own_bias = bias_of(tile)
    near_bias = bias_of(near_tile)

    def keep(h, carry):
        arrived[h, me] = out_blocks[h, me]
        return carry

    lax.fori_loop(0, heads_here, keep, 0)

    def scores_of(query_rows, key_head):
        return lax.dot_general(
            query_rows, key_head, (((1,), (1,)), ((), ())), preferred_element_type=jnp.float32
        )

    def with_ones(value_head):
        return jnp.concatenate([value_head, jnp.ones(value_head.shape, value_head.dtype)], axis=1)

    def to_row(spread):
        return spread.T[:1]

    def to_column(row):
        return jnp.broadcast_to(row, (HS, row.shape[1])).T

    def attend(queries, h, emit, listed_at=None, bias=None):
        key_head = own[0, h]
        value_head = with_ones(own[1, h])
        if bias is not None:
            cached_key = arrived[h, :, listed_at, 0].reshape(-1, HS)
            cached_value = with_ones(arrived[h, :, listed_at, 1].reshape(-1, HS))
        for at in range(tok_rows // Q_ROWS):
            rows = pl.ds(at * Q_ROWS, Q_ROWS)
            query_rows = queries[h, rows, :]
            scores = scores_of(query_rows, key_head)
            row_top = jnp.max(scores, axis=1, keepdims=True)
            if bias is not None:
                cached_scores = scores_of(query_rows, cached_key) + bias
                row_top = jnp.maximum(row_top, jnp.max(cached_scores, axis=1, keepdims=True))
            row_exp = jnp.exp2((scores - row_top) * EXP_SCALE).astype(jnp.bfloat16)
            part = jnp.dot(row_exp, value_head, preferred_element_type=jnp.float32)
            if bias is not None:
                row_exp = jnp.exp2((cached_scores - row_top) * EXP_SCALE).astype(jnp.bfloat16)
                part = part + jnp.dot(row_exp, cached_value, preferred_element_type=jnp.float32)
            total = part[:, HS:]
            emit(rows, part[:, :HS] / total, row_top * EXP_SCALE + jnp.log2(total))

    def emit_to(part_ref, log_ref, h):
        def emit(rows, part, log):
            part_ref[h, rows, :] = part.astype(part_ref.dtype)
            log_ref[h, :, rows] = to_row(log)

        return emit

    def emit_joined(h):
        def emit(rows, part, log):
            other = to_column(far_log[h, :, rows])
            log_top = jnp.maximum(log, other)
            weight = jnp.exp2(log - log_top)
            other_weight = jnp.exp2(other - log_top)
            both = weight + other_weight
            joined = (part * weight + far_part[h, rows, :].astype(jnp.float32) * other_weight) / both
            sent_part[h, rows, :] = joined.astype(sent_part.dtype)
            sent_log[h, :, rows] = to_row(log_top + jnp.log2(both))

        return emit

    def wait_own(h):
        for which in range(2):
            own_load(h, which).wait()

    def take_wave(wave):
        def take(offset, carry):
            block_arrival(wave, offset).wait_recv()
            return carry

        lax.fori_loop(1, side, take, 0)

    def turn(at, carry):
        @pl.when(at < heads_here)
        def _():
            wait_own(at)

            @pl.when(is_end)
            def _():
                query_copy(at).wait_recv()
                relay_copy(at).start()

            @pl.when(is_mid)
            def _():
                relay_copy(at).wait_recv()
                attend(q_far, at, emit_to(far_part, far_log, at))
                for which in range(2):
                    far_copy(at, which).start()

        @pl.when(at >= LAG)
        def _():
            h = at - LAG
            for wave in range(waves):

                @pl.when(h == wave * wave_heads)
                def _(wave=wave):
                    take_wave(wave)

            @pl.when(is_mid)
            def _():
                query_copy(h).wait_recv()
                attend(q_near, h, emit_to(sent_part, sent_log, h), 1, near_bias)

            @pl.when(is_end)
            def _():
                for which in range(2):
                    far_copy(h, which).wait_recv()
                attend(q_near, h, emit_joined(h), 1, near_bias)

            for which in range(2):
                part_copy(h, which).start()
            query_load(h).wait()
            attend(q_own, h, emit_to(own_part, own_log, h), 0, own_bias)

        return carry

    lax.fori_loop(0, heads_here + LAG, turn, 0)

    def join(h, carry):
        for which in range(2):
            part_copy(h, which).wait_recv()
        for at in range(tok_rows // Q_ROWS):
            rows = pl.ds(at * Q_ROWS, Q_ROWS)
            log, other = own_log[h, :, rows], got_log[h, :, rows]
            log_top = jnp.maximum(log, other)
            weight, other_weight = jnp.exp2(log - log_top), jnp.exp2(other - log_top)
            share = to_column(weight / (weight + other_weight))
            got = got_part[h, rows, :].astype(jnp.float32)
            result[h, rows, :] = (got + share * (own_part[h, rows, :] - got)).astype(result.dtype)
        result_store(h).start()
        return carry

    lax.fori_loop(0, heads_here, join, 0)

    def finish(h, carry):
        query_copy(h).wait_send()
        for which in range(2):
            part_copy(h, which).wait_send()

        @pl.when(is_end)
        def _():
            relay_copy(h).wait_send()

        @pl.when(is_mid)
        def _():
            for which in range(2):
                far_copy(h, which).wait_send()

        return carry

    def finish_blocks(offset, carry):
        for wave in range(waves):
            block_copy(wave, offset).wait_send()
        return carry

    def finish_stores(h, carry):
        result_store(h).wait()
        return carry

    lax.fori_loop(1, side, finish_blocks, 0)
    lax.fori_loop(0, heads_here, finish, 0)
    lax.fori_loop(0, heads_here, finish_stores, 0)


def kernel(
    tiles, groups, list_ref, count_ref, q_hbm, k_ref, v_ref, cache_k, cache_v, o_hbm,
    q_own, own, cache, result, out_blocks, near, far, arrived, acc, top, total,
    near_send, near_recv, far_send, far_recv, block_send, block_recv,
    q_sem, own_sem, cache_sem, result_sem,
):
    owners = tiles * groups
    tok_rows, col_width = k_ref.shape
    per_owner, block_rows, _ = cache_k.shape
    listed = list_ref.shape[1]
    heads_here = col_width // HS
    relays = tiles == 4
    video = lax.axis_index("dp")
    tile = lax.axis_index("space")
    group = lax.axis_index("heads")
    me = tile * groups + group
    odd = lax.rem(tile, 2)
    pair = tile + 1 - 2 * odd
    is_end = jnp.logical_or(tile == 0, tile == tiles - 1)
    is_mid = jnp.logical_not(is_end)
    across = lax.rem(tile + 2, tiles) if relays else tile - 1 + 2 * odd

    def columns(h):
        return pl.ds(pl.multiple_of(h * HS, HS), HS)

    def cache_load(which):
        return pltpu.make_async_copy(
            (cache_k, cache_v)[which], cache.at[which], cache_sem.at[which]
        )

    def query_load(h):
        return pltpu.make_async_copy(q_hbm.at[:, columns(h)], q_own.at[h], q_sem.at[h])

    def own_load(h, which):
        return pltpu.make_async_copy(
            (k_ref, v_ref)[which].at[:, columns(h)], own.at[which, h], own_sem.at[which, h]
        )

    def result_store(h):
        return pltpu.make_async_copy(result.at[h], o_hbm.at[:, columns(h)], result_sem.at[h])

    def start_loads(h, carry):
        query_load(h).start()
        for which in range(2):
            own_load(h, which).start()
        return carry

    for which in range(2):
        cache_load(which).start()
    lax.fori_loop(0, heads_here, start_loads, 0)

    def peer(offset):
        other = lax.rem(me + offset, owners)
        return other, (video, other // groups, lax.rem(other, groups))

    barrier = pltpu.get_barrier_semaphore()

    def announce(offset, carry):
        _, device = peer(offset)
        pl.semaphore_signal(barrier, inc=1, device_id=device, device_id_type=MESH)
        return carry

    lax.fori_loop(1, owners, announce, 0)
    pl.semaphore_wait(barrier, owners - 1)

    def block_copy(offset):
        other, device = peer(offset)
        return pltpu.make_async_remote_copy(
            src_ref=out_blocks.at[other],
            dst_ref=arrived.at[me],
            send_sem=block_send.at[offset],
            recv_sem=block_recv.at[me],
            device_id=device,
            device_id_type=MESH,
        )

    def block_arrival(offset):
        other, device = peer(offset)
        return pltpu.make_async_remote_copy(
            src_ref=out_blocks.at[other],
            dst_ref=arrived.at[other],
            send_sem=block_send.at[offset],
            recv_sem=block_recv.at[other],
            device_id=device,
            device_id_type=MESH,
        )

    def near_copy(h, which):
        source = (k_ref, v_ref)[which]
        return pltpu.make_async_remote_copy(
            src_ref=source.at[:, columns(h)],
            dst_ref=near.at[which, h],
            send_sem=near_send.at[which, h],
            recv_sem=near_recv.at[which, h],
            device_id=(video, pair, group),
            device_id_type=MESH,
        )

    def far_copy(h, which):
        source = near.at[which, h] if relays else (k_ref, v_ref)[which].at[:, columns(h)]
        return pltpu.make_async_remote_copy(
            src_ref=source,
            dst_ref=far.at[which, h],
            send_sem=far_send.at[which, h],
            recv_sem=far_recv.at[which, h],
            device_id=(video, across, group),
            device_id_type=MESH,
        )

    def start_blocks(offset, carry):
        block_copy(offset).start()
        return carry

    def start_near(h, carry):
        for which in range(2):
            near_copy(h, which).start()
        return carry

    def start_far(h, carry):
        for which in range(2):
            far_copy(h, which).start()
        return carry

    lax.fori_loop(0, heads_here // 2, start_near, 0)
    for which in range(2):
        cache_load(which).wait()

    def pack(to_tile, carry):
        def pick(m, state):
            seen, *ids = state
            block = list_ref[to_tile, m]
            mine = jnp.logical_and(block // per_owner == me, m < count_ref[to_tile])
            ids = [
                jnp.where(jnp.logical_and(mine, seen == slot), lax.rem(block, per_owner), ids[slot])
                for slot in range(CAP)
            ]
            return (seen + mine.astype(jnp.int32), *ids)

        zero = jnp.int32(0)
        _, *ids = lax.fori_loop(0, listed, pick, (zero,) * (CAP + 1))
        for which in range(2):
            for slot in range(CAP):
                block = cache[which, ids[slot]]
                for to_group in range(groups):
                    out_blocks[
                        to_tile * groups + to_group, which, pl.ds(slot * block_rows, block_rows), :
                    ] = block[:, to_group * col_width : (to_group + 1) * col_width]
        return carry

    lax.fori_loop(0, tiles, pack, 0)
    lax.fori_loop(1, owners, start_blocks, 0)
    lax.fori_loop(heads_here // 2, heads_here, start_near, 0)
    if not relays:

        @pl.when(is_mid)
        def _():
            lax.fori_loop(0, heads_here, start_far, 0)

    slots_wide = owners * CAP * block_rows
    lane = lax.broadcasted_iota(jnp.int32, (1, slots_wide), 1)
    lane_owner = lane // (CAP * block_rows)
    lane_slot = lax.rem(lane // block_rows, CAP)

    def hold(m, held):
        live = m < count_ref[tile]
        owner = jnp.where(live, list_ref[tile, m] // per_owner, -1)
        return held + (lane_owner == owner).astype(jnp.int32)

    held = lax.fori_loop(0, listed, hold, jnp.zeros((1, slots_wide), jnp.int32))
    bias_row = jnp.where(lane_slot < held, 0.0, -jnp.inf).astype(jnp.float32)

    arrived[me] = out_blocks[me]

    def step(h, key_head, value_head, first=False, bias=None, last=False):
        for at in range(tok_rows // Q_ROWS):
            rows = pl.ds(at * Q_ROWS, Q_ROWS)
            scores = lax.dot_general(
                q_own[h, rows, :], key_head, (((1,), (1,)), ((), ())),
                preferred_element_type=jnp.float32,
            )
            if bias is not None:
                scores = scores + bias
            row_top = jnp.max(scores, axis=1, keepdims=True)
            if not first:
                old_top = top[h, rows, :]
                row_top = jnp.maximum(row_top, old_top)
            row_exp = jnp.exp2((scores - row_top) * EXP_SCALE)
            row_sum = jnp.sum(row_exp, axis=1, keepdims=True)
            part = jnp.dot(
                row_exp.astype(jnp.bfloat16), value_head, preferred_element_type=jnp.float32
            )
            if not first:
                shrink = jnp.exp2((old_top - row_top) * EXP_SCALE)
                row_sum = row_sum + total[h, rows, :] * shrink
                part = part + acc[h, rows, :] * shrink
            top[h, rows, :] = row_top
            total[h, rows, :] = row_sum
            acc[h, rows, :] = part

    def near_step(h):
        for which in range(2):
            near_copy(h, which).wait_recv()
            if relays:

                @pl.when(is_end)
                def _(which=which):
                    far_copy(h, which).start()

        step(h, near[0, h], near[1, h])

    def first_pass(h, carry):
        query_load(h).wait()
        for which in range(2):
            own_load(h, which).wait()
        step(h, own[0, h], own[1, h], first=True)

        @pl.when(is_end)
        def _():
            near_step(h)

        return carry

    lax.fori_loop(0, heads_here, first_pass, 0)

    def take_blocks(offset, carry):
        block_arrival(offset).wait_recv()
        return carry

    lax.fori_loop(1, owners, take_blocks, 0)

    def second_pass(h, carry):
        cached = [arrived[:, which, :, columns(h)].reshape(-1, HS) for which in range(2)]
        step(h, cached[0], cached[1], bias=bias_row)

        @pl.when(is_mid)
        def _():
            near_step(h)
            for which in range(2):
                far_copy(h, which).wait_recv()
            step(h, far[0, h], far[1, h])

        result[h] = (acc[h] / total[h]).astype(result.dtype)
        result_store(h).start()
        return carry

    lax.fori_loop(0, heads_here, second_pass, 0)

    def finish_blocks(offset, carry):
        block_copy(offset).wait_send()
        return carry

    def finish_near(h, carry):
        result_store(h).wait()
        for which in range(2):
            near_copy(h, which).wait_send()
        return carry

    def finish_far(h, carry):
        for which in range(2):
            far_copy(h, which).wait_send()
        return carry

    lax.fori_loop(1, owners, finish_blocks, 0)
    lax.fori_loop(0, heads_here, finish_near, 0)

    @pl.when(is_end if relays else is_mid)
    def _():
        lax.fori_loop(0, heads_here, finish_far, 0)


def local(queries, keys, values, cache_keys, cache_values, block_list, block_counts):
    tile_count = lax.axis_size("space")
    groups = lax.axis_size("heads")
    tok_rows, col_width = queries.shape
    per_owner, block_rows, full_width = cache_keys.shape
    owners = tile_count * groups
    heads_here = col_width // HS
    scalars = pl.BlockSpec(memory_space=pltpu.SMEM)
    whole = pl.BlockSpec(memory_space=pl.ANY)
    tile_shape = (2, heads_here, tok_rows, HS)
    blocks_shape = (owners, 2, CAP * block_rows, col_width)
    per_head = pltpu.SemaphoreType.DMA((2, heads_here))
    one_each = pltpu.SemaphoreType.DMA((heads_here,))
    per_owner_sem = pltpu.SemaphoreType.DMA((owners,))
    return pl.pallas_call(
        functools.partial(kernel, tile_count, groups),
        out_shape=jax.ShapeDtypeStruct(queries.shape, queries.dtype),
        in_specs=[scalars] * 2 + [whole] * 5,
        out_specs=whole,
        scratch_shapes=[
            pltpu.VMEM(tile_shape[1:], jnp.bfloat16),
            pltpu.VMEM(tile_shape, jnp.bfloat16),
            pltpu.VMEM((2, *cache_keys.shape), jnp.bfloat16),
            pltpu.VMEM(tile_shape[1:], jnp.bfloat16),
            pltpu.VMEM(blocks_shape, jnp.bfloat16),
            pltpu.VMEM(tile_shape, jnp.bfloat16),
            pltpu.VMEM(tile_shape, jnp.bfloat16),
            pltpu.VMEM(blocks_shape, jnp.bfloat16),
            pltpu.VMEM((heads_here, tok_rows, HS), jnp.float32),
            pltpu.VMEM((heads_here, tok_rows, 1), jnp.float32),
            pltpu.VMEM((heads_here, tok_rows, 1), jnp.float32),
            per_head, per_head, per_head, per_head, per_owner_sem, per_owner_sem,
            one_each, per_head, pltpu.SemaphoreType.DMA((2,)), one_each,
        ],
        compiler_params=pltpu.CompilerParams(
            collective_id=0, has_side_effects=True, vmem_limit_bytes=60 * 1024 * 1024
        ),
    )(block_list, block_counts, queries, keys, values, cache_keys, cache_values)


def local_sides(queries, keys, values, cache_keys, cache_values, block_list, block_counts):
    groups = lax.axis_size("heads")
    tok_rows, col_width = queries.shape
    _, block_rows, _ = cache_keys.shape
    heads_here = col_width // HS
    waves = 2 if heads_here % 2 == 0 else 1
    side = 2 * groups
    scalars = pl.BlockSpec(memory_space=pltpu.SMEM)
    whole = pl.BlockSpec(memory_space=pl.ANY)
    rows_shape = (heads_here, tok_rows, HS)
    blocks_shape = (heads_here, side, 2, 2, CAP * block_rows, HS)
    rows16 = pltpu.VMEM(rows_shape, jnp.bfloat16)
    logs = pltpu.VMEM((heads_here, 1, tok_rows), jnp.float32)
    per_head = pltpu.SemaphoreType.DMA((2, heads_here))
    one_each = pltpu.SemaphoreType.DMA((heads_here,))
    per_peer = pltpu.SemaphoreType.DMA((waves, side))
    return pl.pallas_call(
        functools.partial(side_kernel, groups, waves),
        out_shape=jax.ShapeDtypeStruct(queries.shape, queries.dtype),
        in_specs=[scalars] * 2 + [whole] * 5,
        out_specs=whole,
        scratch_shapes=[
            rows16,
            pltpu.VMEM((2, *rows_shape), jnp.bfloat16),
            rows16, rows16,
            pltpu.VMEM((2, *cache_keys.shape), jnp.bfloat16),
            pltpu.VMEM(blocks_shape, jnp.bfloat16),
            pltpu.VMEM(blocks_shape, jnp.bfloat16),
            pltpu.VMEM(rows_shape, jnp.float32), logs,
            rows16, logs, rows16, logs, rows16, logs, rows16,
            one_each, one_each, one_each, one_each, per_head, per_head, per_head, per_head,
            per_peer, per_peer, one_each, per_head, pltpu.SemaphoreType.DMA((2,)), one_each,
        ],
        compiler_params=pltpu.CompilerParams(
            collective_id=1, has_side_effects=True, vmem_limit_bytes=60 * 1024 * 1024
        ),
    )(block_list, block_counts, queries, keys, values, cache_keys, cache_values)


def solution(mesh):
    placed = (
        P(("dp", "space"), "heads"),
        P(("dp", "space"), "heads"),
        P(("dp", "space"), "heads"),
        P(("dp", "space", "heads"), None, None),
        P(("dp", "space", "heads"), None, None),
        P("dp", None),
        P("dp"),
    )
    body = local_sides if mesh.shape["space"] == 4 else local
    return jax.shard_map(
        body, mesh=mesh, in_specs=placed, out_specs=P(("dp", "space"), "heads"), check_vma=False
    )
```

```python
import functools

import jax
import jax.numpy as jnp
from jax import lax
from jax.experimental import pallas as pl
from jax.experimental.pallas import tpu as pltpu
from jax.sharding import PartitionSpec as P

HS = 128
CAP = 2
Q_ROWS = 256
LAG = 2
EXP_SCALE = HS ** (-0.5) * 1.4426950408889634
MESH = pl.DeviceIdType.MESH


def side_kernel(
    groups, waves, list_ref, count_ref, q_hbm, k_ref, v_ref, cache_k, cache_v, o_ref,
    q_own, own, q_near, q_far, cache, out_blocks, arrived,
    own_part, own_log, sent_part, sent_log, got_part, got_log, far_part, far_log,
    q_send, q_recv, relay_send, relay_recv, part_send, part_recv, far_send, far_recv,
    block_send, block_recv, q_sem, own_sem, cache_sem,
):
    tok_rows, col_width = k_ref.shape
    per_owner, block_rows, _ = cache_k.shape
    listed = list_ref.shape[1]
    heads_here = col_width // HS
    wave_heads = heads_here // waves
    side = 2 * groups
    video = lax.axis_index("dp")
    tile = lax.axis_index("space")
    group = lax.axis_index("heads")
    odd = lax.rem(tile, 2)
    tile_y = tile // 2
    near_tile = tile + 1 - 2 * odd
    far_tile = lax.rem(tile + 2, 4)
    me = tile_y * groups + group
    is_end = jnp.logical_or(tile == 0, tile == 3)
    is_mid = jnp.logical_not(is_end)
    near_device = (video, near_tile, group)
    far_device = (video, far_tile, group)

    def columns(h):
        return pl.ds(pl.multiple_of(h * HS, HS), HS)

    def cache_load(which):
        return pltpu.make_async_copy(
            (cache_k, cache_v)[which], cache.at[which], cache_sem.at[which]
        )

    def query_load(h):
        return pltpu.make_async_copy(q_hbm.at[:, columns(h)], q_own.at[h], q_sem.at[h])

    def own_load(h, which):
        return pltpu.make_async_copy(
            (k_ref, v_ref)[which].at[:, columns(h)], own.at[which, h], own_sem.at[which, h]
        )

    def remote(src, dst, send_sem, recv_sem, device):
        return pltpu.make_async_remote_copy(
            src_ref=src, dst_ref=dst, send_sem=send_sem, recv_sem=recv_sem,
            device_id=device, device_id_type=MESH,
        )

    def query_copy(h):
        return remote(
            q_hbm.at[:, columns(h)], q_near.at[h], q_send.at[h], q_recv.at[h], near_device
        )

    def relay_copy(h):
        return remote(q_near.at[h], q_far.at[h], relay_send.at[h], relay_recv.at[h], far_device)

    def part_copy(h, which):
        src, dst = ((sent_part, got_part), (sent_log, got_log))[which]
        return remote(
            src.at[h], dst.at[h], part_send.at[which, h], part_recv.at[which, h], near_device
        )

    def far_copy(h, which):
        buffer = (far_part, far_log)[which]
        return remote(
            buffer.at[h], buffer.at[h], far_send.at[which, h], far_recv.at[which, h], far_device
        )

    def peer(offset):
        other = lax.rem(me + offset, side)
        return other, (video, odd + 2 * (other // groups), lax.rem(other, groups))

    def wave_part(wave):
        return pl.ds(wave * wave_heads, wave_heads)

    def block_copy(wave, offset):
        other, device = peer(offset)
        return remote(
            out_blocks.at[wave_part(wave), other], arrived.at[wave_part(wave), me],
            block_send.at[wave, offset], block_recv.at[wave, me], device,
        )

    def block_arrival(wave, offset):
        other, device = peer(offset)
        return remote(
            out_blocks.at[wave_part(wave), other], arrived.at[wave_part(wave), other],
            block_send.at[wave, offset], block_recv.at[wave, other], device,
        )

    def start_loads(h, carry):
        query_load(h).start()
        for which in range(2):
            own_load(h, which).start()
        return carry

    for which in range(2):
        cache_load(which).start()

    barrier = pltpu.get_barrier_semaphore()

    def announce(offset, carry):
        _, device = peer(offset)
        pl.semaphore_signal(barrier, inc=1, device_id=device, device_id_type=MESH)
        return carry

    pl.semaphore_signal(barrier, inc=1, device_id=near_device, device_id_type=MESH)
    lax.fori_loop(1, side, announce, 0)
    lax.fori_loop(0, heads_here, start_loads, 0)
    pl.semaphore_wait(barrier, side)

    def start_queries(h, carry):
        query_copy(h).start()
        return carry

    lax.fori_loop(0, heads_here, start_queries, 0)
    for which in range(2):
        cache_load(which).wait()

    def pack(to_tile, carry):
        def pick(m, state):
            seen, *ids = state
            block = list_ref[to_tile, m]
            owner = block // per_owner
            mine = jnp.logical_and(owner == tile * groups + group, m < count_ref[to_tile])
            ids = [
                jnp.where(jnp.logical_and(mine, seen == slot), lax.rem(block, per_owner), ids[slot])
                for slot in range(CAP)
            ]
            return (seen + mine.astype(jnp.int32), *ids)

        zero = jnp.int32(0)
        _, *ids = lax.fori_loop(0, listed, pick, (zero,) * (CAP + 1))
        crossed = lax.rem(to_tile + odd, 2)
        for which in range(2):
            for slot in range(CAP):
                block = cache[which, ids[slot]]
                for to_group in range(groups):
                    for h in range(heads_here):
                        start = to_group * col_width + h * HS
                        out_blocks[
                            h, to_tile // 2 * groups + to_group, crossed, which,
                            pl.ds(slot * block_rows, block_rows), :
                        ] = block[:, start : start + HS]
        return carry

    lax.fori_loop(0, 4, pack, 0)

    def start_blocks(wave):
        def start(offset, carry):
            block_copy(wave, offset).start()
            return carry

        lax.fori_loop(1, side, start, 0)

    for wave in range(waves):
        start_blocks(wave)

    slots_wide = side * CAP * block_rows
    lane = lax.broadcasted_iota(jnp.int32, (1, slots_wide), 1)
    lane_side = lane // (CAP * block_rows)
    lane_owner = (odd + 2 * (lane_side // groups)) * groups + lax.rem(lane_side, groups)
    lane_slot = lax.rem(lane // block_rows, CAP)

    def bias_of(list_tile):
        def hold(m, held):
            live = m < count_ref[list_tile]
            owner = jnp.where(live, list_ref[list_tile, m] // per_owner, -1)
            return held + (lane_owner == owner).astype(jnp.int32)

        held = lax.fori_loop(0, listed, hold, jnp.zeros((1, slots_wide), jnp.int32))
        return jnp.where(lane_slot < held, 0.0, -jnp.inf).astype(jnp.float32)

    own_bias = bias_of(tile)
    near_bias = bias_of(near_tile)

    def keep(h, carry):
        arrived[h, me] = out_blocks[h, me]
        return carry

    lax.fori_loop(0, heads_here, keep, 0)

    def scores_of(query_rows, key_head):
        return lax.dot_general(
            query_rows, key_head, (((1,), (1,)), ((), ())), preferred_element_type=jnp.float32
        )

    def with_ones(value_head):
        return jnp.concatenate([value_head, jnp.ones(value_head.shape, value_head.dtype)], axis=1)

    def to_row(spread):
        return spread.T[:1]

    def to_column(row):
        return jnp.broadcast_to(row, (HS, row.shape[1])).T

    def attend(queries, h, emit, listed_at=None, bias=None):
        key_head = own[0, h]
        value_head = with_ones(own[1, h])
        if bias is not None:
            cached_key = arrived[h, :, listed_at, 0].reshape(-1, HS)
            cached_value = with_ones(arrived[h, :, listed_at, 1].reshape(-1, HS))
        for at in range(tok_rows // Q_ROWS):
            rows = pl.ds(at * Q_ROWS, Q_ROWS)
            query_rows = queries[h, rows, :]
            scores = scores_of(query_rows, key_head)
            row_top = jnp.max(scores, axis=1, keepdims=True)
            if bias is not None:
                cached_scores = scores_of(query_rows, cached_key) + bias
                row_top = jnp.maximum(row_top, jnp.max(cached_scores, axis=1, keepdims=True))
            row_exp = jnp.exp2((scores - row_top) * EXP_SCALE).astype(jnp.bfloat16)
            part = jnp.dot(row_exp, value_head, preferred_element_type=jnp.float32)
            if bias is not None:
                row_exp = jnp.exp2((cached_scores - row_top) * EXP_SCALE).astype(jnp.bfloat16)
                part = part + jnp.dot(row_exp, cached_value, preferred_element_type=jnp.float32)
            total = part[:, HS:]
            emit(rows, part[:, :HS] / total, row_top * EXP_SCALE + jnp.log2(total))

    def emit_to(part_ref, log_ref, h):
        def emit(rows, part, log):
            part_ref[h, rows, :] = part.astype(part_ref.dtype)
            log_ref[h, :, rows] = to_row(log)

        return emit

    def emit_joined(h):
        def emit(rows, part, log):
            other = to_column(far_log[h, :, rows])
            log_top = jnp.maximum(log, other)
            weight = jnp.exp2(log - log_top)
            other_weight = jnp.exp2(other - log_top)
            both = weight + other_weight
            joined = (part * weight + far_part[h, rows, :].astype(jnp.float32) * other_weight) / both
            sent_part[h, rows, :] = joined.astype(sent_part.dtype)
            sent_log[h, :, rows] = to_row(log_top + jnp.log2(both))

        return emit

    def wait_own(h):
        for which in range(2):
            own_load(h, which).wait()

    def take_wave(wave):
        def take(offset, carry):
            block_arrival(wave, offset).wait_recv()
            return carry

        lax.fori_loop(1, side, take, 0)

    def turn(at, carry):
        @pl.when(at < heads_here)
        def _():
            wait_own(at)

            @pl.when(is_end)
            def _():
                query_copy(at).wait_recv()
                relay_copy(at).start()

            @pl.when(is_mid)
            def _():
                relay_copy(at).wait_recv()
                attend(q_far, at, emit_to(far_part, far_log, at))
                for which in range(2):
                    far_copy(at, which).start()

        @pl.when(at >= LAG)
        def _():
            h = at - LAG
            for wave in range(waves):

                @pl.when(h == wave * wave_heads)
                def _(wave=wave):
                    take_wave(wave)

            @pl.when(is_mid)
            def _():
                query_copy(h).wait_recv()
                attend(q_near, h, emit_to(sent_part, sent_log, h), 1, near_bias)

            @pl.when(is_end)
            def _():
                for which in range(2):
                    far_copy(h, which).wait_recv()
                attend(q_near, h, emit_joined(h), 1, near_bias)

            for which in range(2):
                part_copy(h, which).start()
            query_load(h).wait()
            attend(q_own, h, emit_to(own_part, own_log, h), 0, own_bias)

        return carry

    lax.fori_loop(0, heads_here + LAG, turn, 0)

    def join(h, carry):
        for which in range(2):
            part_copy(h, which).wait_recv()
        for at in range(tok_rows // Q_ROWS):
            rows = pl.ds(at * Q_ROWS, Q_ROWS)
            log, other = own_log[h, :, rows], got_log[h, :, rows]
            log_top = jnp.maximum(log, other)
            weight, other_weight = jnp.exp2(log - log_top), jnp.exp2(other - log_top)
            share = to_column(weight / (weight + other_weight))
            got = got_part[h, rows, :].astype(jnp.float32)
            o_ref[rows, columns(h)] = (got + share * (own_part[h, rows, :] - got)).astype(o_ref.dtype)
        return carry

    lax.fori_loop(0, heads_here, join, 0)

    def finish(h, carry):
        query_copy(h).wait_send()
        for which in range(2):
            part_copy(h, which).wait_send()

        @pl.when(is_end)
        def _():
            relay_copy(h).wait_send()

        @pl.when(is_mid)
        def _():
            for which in range(2):
                far_copy(h, which).wait_send()

        return carry

    def finish_blocks(offset, carry):
        for wave in range(waves):
            block_copy(wave, offset).wait_send()
        return carry

    lax.fori_loop(1, side, finish_blocks, 0)
    lax.fori_loop(0, heads_here, finish, 0)


def kernel(
    tiles, groups, list_ref, count_ref, q_hbm, k_ref, v_ref, cache_k, cache_v, o_hbm,
    q_own, own, cache, result, out_blocks, near, far, arrived, acc, top, total,
    near_send, near_recv, far_send, far_recv, block_send, block_recv,
    q_sem, own_sem, cache_sem, result_sem,
):
    owners = tiles * groups
    tok_rows, col_width = k_ref.shape
    per_owner, block_rows, _ = cache_k.shape
    listed = list_ref.shape[1]
    heads_here = col_width // HS
    relays = tiles == 4
    video = lax.axis_index("dp")
    tile = lax.axis_index("space")
    group = lax.axis_index("heads")
    me = tile * groups + group
    odd = lax.rem(tile, 2)
    pair = tile + 1 - 2 * odd
    is_end = jnp.logical_or(tile == 0, tile == tiles - 1)
    is_mid = jnp.logical_not(is_end)
    across = lax.rem(tile + 2, tiles) if relays else tile - 1 + 2 * odd

    def columns(h):
        return pl.ds(pl.multiple_of(h * HS, HS), HS)

    def cache_load(which):
        return pltpu.make_async_copy(
            (cache_k, cache_v)[which], cache.at[which], cache_sem.at[which]
        )

    def query_load(h):
        return pltpu.make_async_copy(q_hbm.at[:, columns(h)], q_own.at[h], q_sem.at[h])

    def own_load(h, which):
        return pltpu.make_async_copy(
            (k_ref, v_ref)[which].at[:, columns(h)], own.at[which, h], own_sem.at[which, h]
        )

    def result_store(h):
        return pltpu.make_async_copy(result.at[h], o_hbm.at[:, columns(h)], result_sem.at[h])

    def start_loads(h, carry):
        query_load(h).start()
        for which in range(2):
            own_load(h, which).start()
        return carry

    for which in range(2):
        cache_load(which).start()
    lax.fori_loop(0, heads_here, start_loads, 0)

    def peer(offset):
        other = lax.rem(me + offset, owners)
        return other, (video, other // groups, lax.rem(other, groups))

    barrier = pltpu.get_barrier_semaphore()

    def announce(offset, carry):
        _, device = peer(offset)
        pl.semaphore_signal(barrier, inc=1, device_id=device, device_id_type=MESH)
        return carry

    lax.fori_loop(1, owners, announce, 0)
    pl.semaphore_wait(barrier, owners - 1)

    def block_copy(offset):
        other, device = peer(offset)
        return pltpu.make_async_remote_copy(
            src_ref=out_blocks.at[other],
            dst_ref=arrived.at[me],
            send_sem=block_send.at[offset],
            recv_sem=block_recv.at[me],
            device_id=device,
            device_id_type=MESH,
        )

    def block_arrival(offset):
        other, device = peer(offset)
        return pltpu.make_async_remote_copy(
            src_ref=out_blocks.at[other],
            dst_ref=arrived.at[other],
            send_sem=block_send.at[offset],
            recv_sem=block_recv.at[other],
            device_id=device,
            device_id_type=MESH,
        )

    def near_copy(h, which):
        source = (k_ref, v_ref)[which]
        return pltpu.make_async_remote_copy(
            src_ref=source.at[:, columns(h)],
            dst_ref=near.at[which, h],
            send_sem=near_send.at[which, h],
            recv_sem=near_recv.at[which, h],
            device_id=(video, pair, group),
            device_id_type=MESH,
        )

    def far_copy(h, which):
        source = near.at[which, h] if relays else (k_ref, v_ref)[which].at[:, columns(h)]
        return pltpu.make_async_remote_copy(
            src_ref=source,
            dst_ref=far.at[which, h],
            send_sem=far_send.at[which, h],
            recv_sem=far_recv.at[which, h],
            device_id=(video, across, group),
            device_id_type=MESH,
        )

    def start_blocks(offset, carry):
        block_copy(offset).start()
        return carry

    def start_near(h, carry):
        for which in range(2):
            near_copy(h, which).start()
        return carry

    def start_far(h, carry):
        for which in range(2):
            far_copy(h, which).start()
        return carry

    lax.fori_loop(0, heads_here // 2, start_near, 0)
    for which in range(2):
        cache_load(which).wait()

    def pack(to_tile, carry):
        def pick(m, state):
            seen, *ids = state
            block = list_ref[to_tile, m]
            mine = jnp.logical_and(block // per_owner == me, m < count_ref[to_tile])
            ids = [
                jnp.where(jnp.logical_and(mine, seen == slot), lax.rem(block, per_owner), ids[slot])
                for slot in range(CAP)
            ]
            return (seen + mine.astype(jnp.int32), *ids)

        zero = jnp.int32(0)
        _, *ids = lax.fori_loop(0, listed, pick, (zero,) * (CAP + 1))
        for which in range(2):
            for slot in range(CAP):
                block = cache[which, ids[slot]]
                for to_group in range(groups):
                    out_blocks[
                        to_tile * groups + to_group, which, pl.ds(slot * block_rows, block_rows), :
                    ] = block[:, to_group * col_width : (to_group + 1) * col_width]
        return carry

    lax.fori_loop(0, tiles, pack, 0)
    lax.fori_loop(1, owners, start_blocks, 0)
    lax.fori_loop(heads_here // 2, heads_here, start_near, 0)
    if not relays:

        @pl.when(is_mid)
        def _():
            lax.fori_loop(0, heads_here, start_far, 0)

    slots_wide = owners * CAP * block_rows
    lane = lax.broadcasted_iota(jnp.int32, (1, slots_wide), 1)
    lane_owner = lane // (CAP * block_rows)
    lane_slot = lax.rem(lane // block_rows, CAP)

    def hold(m, held):
        live = m < count_ref[tile]
        owner = jnp.where(live, list_ref[tile, m] // per_owner, -1)
        return held + (lane_owner == owner).astype(jnp.int32)

    held = lax.fori_loop(0, listed, hold, jnp.zeros((1, slots_wide), jnp.int32))
    bias_row = jnp.where(lane_slot < held, 0.0, -jnp.inf).astype(jnp.float32)

    arrived[me] = out_blocks[me]

    def step(h, key_head, value_head, first=False, bias=None, last=False):
        for at in range(tok_rows // Q_ROWS):
            rows = pl.ds(at * Q_ROWS, Q_ROWS)
            scores = lax.dot_general(
                q_own[h, rows, :], key_head, (((1,), (1,)), ((), ())),
                preferred_element_type=jnp.float32,
            )
            if bias is not None:
                scores = scores + bias
            row_top = jnp.max(scores, axis=1, keepdims=True)
            if not first:
                old_top = top[h, rows, :]
                row_top = jnp.maximum(row_top, old_top)
            row_exp = jnp.exp2((scores - row_top) * EXP_SCALE)
            row_sum = jnp.sum(row_exp, axis=1, keepdims=True)
            part = jnp.dot(
                row_exp.astype(jnp.bfloat16), value_head, preferred_element_type=jnp.float32
            )
            if not first:
                shrink = jnp.exp2((old_top - row_top) * EXP_SCALE)
                row_sum = row_sum + total[h, rows, :] * shrink
                part = part + acc[h, rows, :] * shrink
            top[h, rows, :] = row_top
            total[h, rows, :] = row_sum
            acc[h, rows, :] = part

    def near_step(h):
        for which in range(2):
            near_copy(h, which).wait_recv()
            if relays:

                @pl.when(is_end)
                def _(which=which):
                    far_copy(h, which).start()

        step(h, near[0, h], near[1, h])

    def first_pass(h, carry):
        query_load(h).wait()
        for which in range(2):
            own_load(h, which).wait()
        step(h, own[0, h], own[1, h], first=True)

        @pl.when(is_end)
        def _():
            near_step(h)

        return carry

    lax.fori_loop(0, heads_here, first_pass, 0)

    def take_blocks(offset, carry):
        block_arrival(offset).wait_recv()
        return carry

    lax.fori_loop(1, owners, take_blocks, 0)

    def second_pass(h, carry):
        cached = [arrived[:, which, :, columns(h)].reshape(-1, HS) for which in range(2)]
        step(h, cached[0], cached[1], bias=bias_row)

        @pl.when(is_mid)
        def _():
            near_step(h)
            for which in range(2):
                far_copy(h, which).wait_recv()
            step(h, far[0, h], far[1, h])

        result[h] = (acc[h] / total[h]).astype(result.dtype)
        result_store(h).start()
        return carry

    lax.fori_loop(0, heads_here, second_pass, 0)

    def finish_blocks(offset, carry):
        block_copy(offset).wait_send()
        return carry

    def finish_near(h, carry):
        result_store(h).wait()
        for which in range(2):
            near_copy(h, which).wait_send()
        return carry

    def finish_far(h, carry):
        for which in range(2):
            far_copy(h, which).wait_send()
        return carry

    lax.fori_loop(1, owners, finish_blocks, 0)
    lax.fori_loop(0, heads_here, finish_near, 0)

    @pl.when(is_end if relays else is_mid)
    def _():
        lax.fori_loop(0, heads_here, finish_far, 0)


def local(queries, keys, values, cache_keys, cache_values, block_list, block_counts):
    tile_count = lax.axis_size("space")
    groups = lax.axis_size("heads")
    tok_rows, col_width = queries.shape
    per_owner, block_rows, full_width = cache_keys.shape
    owners = tile_count * groups
    heads_here = col_width // HS
    scalars = pl.BlockSpec(memory_space=pltpu.SMEM)
    whole = pl.BlockSpec(memory_space=pl.ANY)
    tile_shape = (2, heads_here, tok_rows, HS)
    blocks_shape = (owners, 2, CAP * block_rows, col_width)
    per_head = pltpu.SemaphoreType.DMA((2, heads_here))
    one_each = pltpu.SemaphoreType.DMA((heads_here,))
    per_owner_sem = pltpu.SemaphoreType.DMA((owners,))
    return pl.pallas_call(
        functools.partial(kernel, tile_count, groups),
        out_shape=jax.ShapeDtypeStruct(queries.shape, queries.dtype),
        in_specs=[scalars] * 2 + [whole] * 5,
        out_specs=whole,
        scratch_shapes=[
            pltpu.VMEM(tile_shape[1:], jnp.bfloat16),
            pltpu.VMEM(tile_shape, jnp.bfloat16),
            pltpu.VMEM((2, *cache_keys.shape), jnp.bfloat16),
            pltpu.VMEM(tile_shape[1:], jnp.bfloat16),
            pltpu.VMEM(blocks_shape, jnp.bfloat16),
            pltpu.VMEM(tile_shape, jnp.bfloat16),
            pltpu.VMEM(tile_shape, jnp.bfloat16),
            pltpu.VMEM(blocks_shape, jnp.bfloat16),
            pltpu.VMEM((heads_here, tok_rows, HS), jnp.float32),
            pltpu.VMEM((heads_here, tok_rows, 1), jnp.float32),
            pltpu.VMEM((heads_here, tok_rows, 1), jnp.float32),
            per_head, per_head, per_head, per_head, per_owner_sem, per_owner_sem,
            one_each, per_head, pltpu.SemaphoreType.DMA((2,)), one_each,
        ],
        compiler_params=pltpu.CompilerParams(
            collective_id=0, has_side_effects=True, vmem_limit_bytes=60 * 1024 * 1024
        ),
    )(block_list, block_counts, queries, keys, values, cache_keys, cache_values)


def local_sides(queries, keys, values, cache_keys, cache_values, block_list, block_counts):
    groups = lax.axis_size("heads")
    tok_rows, col_width = queries.shape
    _, block_rows, _ = cache_keys.shape
    heads_here = col_width // HS
    waves = 2 if heads_here % 2 == 0 else 1
    side = 2 * groups
    scalars = pl.BlockSpec(memory_space=pltpu.SMEM)
    whole = pl.BlockSpec(memory_space=pl.ANY)
    rows_shape = (heads_here, tok_rows, HS)
    blocks_shape = (heads_here, side, 2, 2, CAP * block_rows, HS)
    rows16 = pltpu.VMEM(rows_shape, jnp.bfloat16)
    logs = pltpu.VMEM((heads_here, 1, tok_rows), jnp.float32)
    per_head = pltpu.SemaphoreType.DMA((2, heads_here))
    one_each = pltpu.SemaphoreType.DMA((heads_here,))
    per_peer = pltpu.SemaphoreType.DMA((waves, side))
    return pl.pallas_call(
        functools.partial(side_kernel, groups, waves),
        out_shape=pltpu.VMEM(queries.shape, queries.dtype),
        in_specs=[scalars] * 2 + [whole] * 5,
        out_specs=pl.BlockSpec(memory_space=pltpu.VMEM),
        scratch_shapes=[
            rows16,
            pltpu.VMEM((2, *rows_shape), jnp.bfloat16),
            rows16, rows16,
            pltpu.VMEM((2, *cache_keys.shape), jnp.bfloat16),
            pltpu.VMEM(blocks_shape, jnp.bfloat16),
            pltpu.VMEM(blocks_shape, jnp.bfloat16),
            pltpu.VMEM(rows_shape, jnp.float32), logs,
            rows16, logs, rows16, logs, rows16, logs,
            one_each, one_each, one_each, one_each, per_head, per_head, per_head, per_head,
            per_peer, per_peer, one_each, per_head, pltpu.SemaphoreType.DMA((2,)),
        ],
        compiler_params=pltpu.CompilerParams(
            collective_id=1, has_side_effects=True, vmem_limit_bytes=60 * 1024 * 1024
        ),
    )(block_list, block_counts, queries, keys, values, cache_keys, cache_values)


def solution(mesh):
    placed = (
        P(("dp", "space"), "heads"),
        P(("dp", "space"), "heads"),
        P(("dp", "space"), "heads"),
        P(("dp", "space", "heads"), None, None),
        P(("dp", "space", "heads"), None, None),
        P("dp", None),
        P("dp"),
    )
    body = local_sides if mesh.shape["space"] == 4 else local
    return jax.shard_map(
        body, mesh=mesh, in_specs=placed, out_specs=P(("dp", "space"), "heads"), check_vma=False
    )
```

```python
import functools

import jax
import jax.numpy as jnp
from jax import lax
from jax.experimental import pallas as pl
from jax.experimental.pallas import tpu as pltpu
from jax.sharding import PartitionSpec as P

HS = 128
CAP = 2
Q_ROWS = 256
END_LAG, MID_LAG = 3, 1
EXP_SCALE = HS ** (-0.5) * 1.4426950408889634
MESH = pl.DeviceIdType.MESH


def side_kernel(
    groups, waves, list_ref, count_ref, q_hbm, k_ref, v_ref, cache_k, cache_v, o_ref,
    q_own, own, q_near, q_far, cache, out_blocks, arrived,
    own_part, own_log, sent_part, sent_log, got_part, got_log, far_part, far_log,
    q_send, q_recv, relay_send, relay_recv, part_send, part_recv, far_send, far_recv,
    block_send, block_recv, q_sem, own_sem, cache_sem,
):
    tok_rows, col_width = k_ref.shape
    per_owner, block_rows, _ = cache_k.shape
    listed = list_ref.shape[1]
    heads_here = col_width // HS
    wave_heads = heads_here // waves
    side = 2 * groups
    video = lax.axis_index("dp")
    tile = lax.axis_index("space")
    group = lax.axis_index("heads")
    odd = lax.rem(tile, 2)
    tile_y = tile // 2
    near_tile = tile + 1 - 2 * odd
    far_tile = lax.rem(tile + 2, 4)
    me = tile_y * groups + group
    is_end = jnp.logical_or(tile == 0, tile == 3)
    is_mid = jnp.logical_not(is_end)
    near_device = (video, near_tile, group)
    far_device = (video, far_tile, group)

    def columns(h):
        return pl.ds(pl.multiple_of(h * HS, HS), HS)

    def cache_load(which):
        return pltpu.make_async_copy(
            (cache_k, cache_v)[which], cache.at[which], cache_sem.at[which]
        )

    def query_load(h):
        return pltpu.make_async_copy(q_hbm.at[:, columns(h)], q_own.at[h], q_sem.at[h])

    def own_load(h, which):
        return pltpu.make_async_copy(
            (k_ref, v_ref)[which].at[:, columns(h)], own.at[which, h], own_sem.at[which, h]
        )

    def remote(src, dst, send_sem, recv_sem, device):
        return pltpu.make_async_remote_copy(
            src_ref=src, dst_ref=dst, send_sem=send_sem, recv_sem=recv_sem,
            device_id=device, device_id_type=MESH,
        )

    def query_copy(h):
        return remote(
            q_hbm.at[:, columns(h)], q_near.at[h], q_send.at[h], q_recv.at[h], near_device
        )

    def relay_copy(h):
        return remote(q_near.at[h], q_far.at[h], relay_send.at[h], relay_recv.at[h], far_device)

    def part_copy(h, which):
        src, dst = ((sent_part, got_part), (sent_log, got_log))[which]
        return remote(
            src.at[h], dst.at[h], part_send.at[which, h], part_recv.at[which, h], near_device
        )

    def far_copy(h, which):
        buffer = (far_part, far_log)[which]
        return remote(
            buffer.at[h], buffer.at[h], far_send.at[which, h], far_recv.at[which, h], far_device
        )

    def peer(offset):
        other = lax.rem(me + offset, side)
        return other, (video, odd + 2 * (other // groups), lax.rem(other, groups))

    def wave_part(wave):
        return pl.ds(wave * wave_heads, wave_heads)

    def block_copy(wave, offset):
        other, device = peer(offset)
        return remote(
            out_blocks.at[wave_part(wave), other], arrived.at[wave_part(wave), me],
            block_send.at[wave, offset], block_recv.at[wave, me], device,
        )

    def block_arrival(wave, offset):
        other, device = peer(offset)
        return remote(
            out_blocks.at[wave_part(wave), other], arrived.at[wave_part(wave), other],
            block_send.at[wave, offset], block_recv.at[wave, other], device,
        )

    def start_loads(h, carry):
        query_load(h).start()
        for which in range(2):
            own_load(h, which).start()
        return carry

    for which in range(2):
        cache_load(which).start()

    barrier = pltpu.get_barrier_semaphore()

    def announce(offset, carry):
        _, device = peer(offset)

        @pl.when(jnp.logical_or(group == 0, offset != groups))
        def _():
            pl.semaphore_signal(barrier, inc=1, device_id=device, device_id_type=MESH)

        return carry

    pl.semaphore_signal(barrier, inc=1, device_id=near_device, device_id_type=MESH)

    @pl.when(group > 0)
    def _():
        pl.semaphore_signal(barrier, inc=1, device_id=far_device, device_id_type=MESH)

    lax.fori_loop(0, heads_here, start_loads, 0)
    earlier = jnp.where(group == 0, 1 + tile_y, 2 + 2 * group)
    pl.semaphore_wait(barrier, earlier)

    def start_queries(h, carry):
        query_copy(h).start()
        return carry

    lax.fori_loop(0, heads_here, start_queries, 0)
    lax.fori_loop(1, side, announce, 0)
    for which in range(2):
        cache_load(which).wait()

    def pack(to_tile, carry):
        def pick(m, state):
            seen, *ids = state
            block = list_ref[to_tile, m]
            owner = block // per_owner
            mine = jnp.logical_and(owner == tile * groups + group, m < count_ref[to_tile])
            ids = [
                jnp.where(jnp.logical_and(mine, seen == slot), lax.rem(block, per_owner), ids[slot])
                for slot in range(CAP)
            ]
            return (seen + mine.astype(jnp.int32), *ids)

        zero = jnp.int32(0)
        _, *ids = lax.fori_loop(0, listed, pick, (zero,) * (CAP + 1))
        crossed = lax.rem(to_tile + odd, 2)
        for which in range(2):
            for slot in range(CAP):
                block = cache[which, ids[slot]]
                for to_group in range(groups):
                    for h in range(heads_here):
                        start = to_group * col_width + h * HS
                        out_blocks[
                            h, to_tile // 2 * groups + to_group, crossed, which,
                            pl.ds(slot * block_rows, block_rows), :
                        ] = block[:, start : start + HS]
        return carry

    lax.fori_loop(0, 4, pack, 0)

    def start_blocks(wave):
        def start(offset, carry):
            block_copy(wave, offset).start()
            return carry

        lax.fori_loop(1, side, start, 0)


    @pl.when(earlier < side)
    def _():
        pl.semaphore_wait(barrier, side - earlier)

    for wave in range(min(waves, 2)):
        start_blocks(wave)

    slots_wide = side * CAP * block_rows
    lane = lax.broadcasted_iota(jnp.int32, (1, slots_wide), 1)
    lane_side = lane // (CAP * block_rows)
    lane_owner = (odd + 2 * (lane_side // groups)) * groups + lax.rem(lane_side, groups)
    lane_slot = lax.rem(lane // block_rows, CAP)

    def bias_of(list_tile):
        def hold(m, held):
            live = m < count_ref[list_tile]
            owner = jnp.where(live, list_ref[list_tile, m] // per_owner, -1)
            return held + (lane_owner == owner).astype(jnp.int32)

        held = lax.fori_loop(0, listed, hold, jnp.zeros((1, slots_wide), jnp.int32))
        return jnp.where(lane_slot < held, 0.0, -jnp.inf).astype(jnp.float32)

    own_bias = bias_of(tile)
    near_bias = bias_of(near_tile)

    def keep(h, carry):
        arrived[h, me] = out_blocks[h, me]
        return carry

    lax.fori_loop(0, heads_here, keep, 0)

    def scores_of(query_rows, key_head):
        return lax.dot_general(
            query_rows, key_head, (((1,), (1,)), ((), ())), preferred_element_type=jnp.float32
        )

    def with_ones(value_head):
        return jnp.concatenate([value_head, jnp.ones(value_head.shape, value_head.dtype)], axis=1)

    def to_row(spread):
        on_diagonal = lax.broadcasted_iota(jnp.int32, (HS, HS), 0) == lax.broadcasted_iota(
            jnp.int32, (HS, HS), 1
        )
        pieces = [
            jnp.sum(jnp.where(on_diagonal, spread[at : at + HS], 0.0), axis=0, keepdims=True)
            for at in range(0, spread.shape[0], HS)
        ]
        return jnp.concatenate(pieces, axis=1)

    def to_column(row):
        return jnp.broadcast_to(row, (HS, row.shape[1])).T

    def attend(queries, h, emit, listed_at=None, bias=None):
        key_head = own[0, h]
        value_head = with_ones(own[1, h])
        if bias is not None:
            cached_key = arrived[h, :, listed_at, 0].reshape(-1, HS)
            cached_value = with_ones(arrived[h, :, listed_at, 1].reshape(-1, HS))
        def scores_at(at):
            query_rows = queries[h, pl.ds(at * Q_ROWS, Q_ROWS), :]
            cached_scores = None if bias is None else scores_of(query_rows, cached_key) + bias
            return scores_of(query_rows, key_head), cached_scores

        steps = tok_rows // Q_ROWS
        ahead = scores_at(0)
        for at in range(steps):
            scores, cached_scores = ahead
            if at + 1 < steps:
                ahead = scores_at(at + 1)
            row_top = jnp.max(scores, axis=1, keepdims=True)
            if bias is not None:
                row_top = jnp.maximum(row_top, jnp.max(cached_scores, axis=1, keepdims=True))
            row_exp = jnp.exp2((scores - row_top) * EXP_SCALE).astype(jnp.bfloat16)
            part = jnp.dot(row_exp, value_head, preferred_element_type=jnp.float32)
            if bias is not None:
                row_exp = jnp.exp2((cached_scores - row_top) * EXP_SCALE).astype(jnp.bfloat16)
                part = part + jnp.dot(row_exp, cached_value, preferred_element_type=jnp.float32)
            total = part[:, HS:]
            rows = pl.ds(at * Q_ROWS, Q_ROWS)
            emit(rows, part[:, :HS] / total, row_top * EXP_SCALE + jnp.log2(total))

    def emit_to(part_ref, log_ref, h):
        def emit(rows, part, log):
            part_ref[h, rows, :] = part.astype(part_ref.dtype)
            log_ref[h, :, rows] = to_row(log)

        return emit

    def emit_joined(h):
        def emit(rows, part, log):
            other = to_column(far_log[h, :, rows])
            log_top = jnp.maximum(log, other)
            weight = jnp.exp2(log - log_top)
            other_weight = jnp.exp2(other - log_top)
            both = weight + other_weight
            joined = (part * weight + far_part[h, rows, :].astype(jnp.float32) * other_weight) / both
            sent_part[h, rows, :] = joined.astype(sent_part.dtype)
            sent_log[h, :, rows] = to_row(log_top + jnp.log2(both))

        return emit

    def wait_own(h):
        for which in range(2):
            own_load(h, which).wait()

    def take_wave(wave):
        def take(offset, carry):
            block_arrival(wave, offset).wait_recv()
            return carry

        lax.fori_loop(1, side, take, 0)

    def near_and_own(h, emit):
        for wave in range(waves):

            @pl.when(h == wave * wave_heads)
            def _(wave=wave):
                take_wave(wave)

        attend(q_near, h, emit, 1, near_bias)
        for which in range(2):
            part_copy(h, which).start()
        query_load(h).wait()
        attend(q_own, h, emit_to(own_part, own_log, h), 0, own_bias)

    def later_waves(at):
        for wave in range(2, waves):

            @pl.when(at == wave_heads * (wave - 1))
            def _(wave=wave):
                start_blocks(wave)

    def end_turn(at, carry):
        later_waves(at)

        @pl.when(at < heads_here)
        def _():
            wait_own(at)
            query_copy(at).wait_recv()
            relay_copy(at).start()

        @pl.when(at >= END_LAG)
        def _():
            h = at - END_LAG
            for which in range(2):
                far_copy(h, which).wait_recv()
            near_and_own(h, emit_joined(h))

        return carry

    def mid_turn(at, carry):
        later_waves(at)

        @pl.when(at < heads_here)
        def _():
            wait_own(at)
            relay_copy(at).wait_recv()
            attend(q_far, at, emit_to(far_part, far_log, at))
            for which in range(2):
                far_copy(at, which).start()

        @pl.when(at >= MID_LAG)
        def _():
            h = at - MID_LAG
            query_copy(h).wait_recv()
            near_and_own(h, emit_to(sent_part, sent_log, h))

        return carry

    @pl.when(is_end)
    def _():
        lax.fori_loop(0, heads_here + END_LAG, end_turn, 0)

    @pl.when(is_mid)
    def _():
        lax.fori_loop(0, heads_here + MID_LAG, mid_turn, 0)

    def join(h, carry):
        for which in range(2):
            part_copy(h, which).wait_recv()
        for at in range(tok_rows // Q_ROWS):
            rows = pl.ds(at * Q_ROWS, Q_ROWS)
            log, other = own_log[h, :, rows], got_log[h, :, rows]
            log_top = jnp.maximum(log, other)
            weight, other_weight = jnp.exp2(log - log_top), jnp.exp2(other - log_top)
            share = to_column(weight / (weight + other_weight))
            got = got_part[h, rows, :].astype(jnp.float32)
            o_ref[rows, columns(h)] = (got + share * (own_part[h, rows, :] - got)).astype(o_ref.dtype)
        return carry

    lax.fori_loop(0, heads_here, join, 0)

    def finish(h, carry):
        query_copy(h).wait_send()
        for which in range(2):
            part_copy(h, which).wait_send()

        @pl.when(is_end)
        def _():
            relay_copy(h).wait_send()

        @pl.when(is_mid)
        def _():
            for which in range(2):
                far_copy(h, which).wait_send()

        return carry

    def finish_blocks(offset, carry):
        for wave in range(waves):
            block_copy(wave, offset).wait_send()
        return carry

    lax.fori_loop(1, side, finish_blocks, 0)
    lax.fori_loop(0, heads_here, finish, 0)


def kernel(
    tiles, groups, list_ref, count_ref, q_hbm, k_ref, v_ref, cache_k, cache_v, o_hbm,
    q_own, own, cache, result, out_blocks, near, far, arrived, acc, top, total,
    near_send, near_recv, far_send, far_recv, block_send, block_recv,
    q_sem, own_sem, cache_sem, result_sem,
):
    owners = tiles * groups
    tok_rows, col_width = k_ref.shape
    per_owner, block_rows, _ = cache_k.shape
    listed = list_ref.shape[1]
    heads_here = col_width // HS
    relays = tiles == 4
    video = lax.axis_index("dp")
    tile = lax.axis_index("space")
    group = lax.axis_index("heads")
    me = tile * groups + group
    odd = lax.rem(tile, 2)
    pair = tile + 1 - 2 * odd
    is_end = jnp.logical_or(tile == 0, tile == tiles - 1)
    is_mid = jnp.logical_not(is_end)
    across = lax.rem(tile + 2, tiles) if relays else tile - 1 + 2 * odd

    def columns(h):
        return pl.ds(pl.multiple_of(h * HS, HS), HS)

    def cache_load(which):
        return pltpu.make_async_copy(
            (cache_k, cache_v)[which], cache.at[which], cache_sem.at[which]
        )

    def query_load(h):
        return pltpu.make_async_copy(q_hbm.at[:, columns(h)], q_own.at[h], q_sem.at[h])

    def own_load(h, which):
        return pltpu.make_async_copy(
            (k_ref, v_ref)[which].at[:, columns(h)], own.at[which, h], own_sem.at[which, h]
        )

    def result_store(h):
        return pltpu.make_async_copy(result.at[h], o_hbm.at[:, columns(h)], result_sem.at[h])

    def start_loads(h, carry):
        query_load(h).start()
        for which in range(2):
            own_load(h, which).start()
        return carry

    for which in range(2):
        cache_load(which).start()
    lax.fori_loop(0, heads_here, start_loads, 0)

    def peer(offset):
        other = lax.rem(me + offset, owners)
        return other, (video, other // groups, lax.rem(other, groups))

    barrier = pltpu.get_barrier_semaphore()

    def announce(offset, carry):
        _, device = peer(offset)
        pl.semaphore_signal(barrier, inc=1, device_id=device, device_id_type=MESH)
        return carry

    lax.fori_loop(1, owners, announce, 0)
    pl.semaphore_wait(barrier, owners - 1)

    def block_copy(offset):
        other, device = peer(offset)
        return pltpu.make_async_remote_copy(
            src_ref=out_blocks.at[other],
            dst_ref=arrived.at[me],
            send_sem=block_send.at[offset],
            recv_sem=block_recv.at[me],
            device_id=device,
            device_id_type=MESH,
        )

    def block_arrival(offset):
        other, device = peer(offset)
        return pltpu.make_async_remote_copy(
            src_ref=out_blocks.at[other],
            dst_ref=arrived.at[other],
            send_sem=block_send.at[offset],
            recv_sem=block_recv.at[other],
            device_id=device,
            device_id_type=MESH,
        )

    def near_copy(h, which):
        source = (k_ref, v_ref)[which]
        return pltpu.make_async_remote_copy(
            src_ref=source.at[:, columns(h)],
            dst_ref=near.at[which, h],
            send_sem=near_send.at[which, h],
            recv_sem=near_recv.at[which, h],
            device_id=(video, pair, group),
            device_id_type=MESH,
        )

    def far_copy(h, which):
        source = near.at[which, h] if relays else (k_ref, v_ref)[which].at[:, columns(h)]
        return pltpu.make_async_remote_copy(
            src_ref=source,
            dst_ref=far.at[which, h],
            send_sem=far_send.at[which, h],
            recv_sem=far_recv.at[which, h],
            device_id=(video, across, group),
            device_id_type=MESH,
        )

    def start_blocks(offset, carry):
        block_copy(offset).start()
        return carry

    def start_near(h, carry):
        for which in range(2):
            near_copy(h, which).start()
        return carry

    def start_far(h, carry):
        for which in range(2):
            far_copy(h, which).start()
        return carry

    lax.fori_loop(0, heads_here // 2, start_near, 0)
    for which in range(2):
        cache_load(which).wait()

    def pack(to_tile, carry):
        def pick(m, state):
            seen, *ids = state
            block = list_ref[to_tile, m]
            mine = jnp.logical_and(block // per_owner == me, m < count_ref[to_tile])
            ids = [
                jnp.where(jnp.logical_and(mine, seen == slot), lax.rem(block, per_owner), ids[slot])
                for slot in range(CAP)
            ]
            return (seen + mine.astype(jnp.int32), *ids)

        zero = jnp.int32(0)
        _, *ids = lax.fori_loop(0, listed, pick, (zero,) * (CAP + 1))
        for which in range(2):
            for slot in range(CAP):
                block = cache[which, ids[slot]]
                for to_group in range(groups):
                    out_blocks[
                        to_tile * groups + to_group, which, pl.ds(slot * block_rows, block_rows), :
                    ] = block[:, to_group * col_width : (to_group + 1) * col_width]
        return carry

    lax.fori_loop(0, tiles, pack, 0)
    lax.fori_loop(1, owners, start_blocks, 0)
    lax.fori_loop(heads_here // 2, heads_here, start_near, 0)
    if not relays:

        @pl.when(is_mid)
        def _():
            lax.fori_loop(0, heads_here, start_far, 0)

    slots_wide = owners * CAP * block_rows
    lane = lax.broadcasted_iota(jnp.int32, (1, slots_wide), 1)
    lane_owner = lane // (CAP * block_rows)
    lane_slot = lax.rem(lane // block_rows, CAP)

    def hold(m, held):
        live = m < count_ref[tile]
        owner = jnp.where(live, list_ref[tile, m] // per_owner, -1)
        return held + (lane_owner == owner).astype(jnp.int32)

    held = lax.fori_loop(0, listed, hold, jnp.zeros((1, slots_wide), jnp.int32))
    bias_row = jnp.where(lane_slot < held, 0.0, -jnp.inf).astype(jnp.float32)

    arrived[me] = out_blocks[me]

    def step(h, key_head, value_head, first=False, bias=None, last=False):
        for at in range(tok_rows // Q_ROWS):
            rows = pl.ds(at * Q_ROWS, Q_ROWS)
            scores = lax.dot_general(
                q_own[h, rows, :], key_head, (((1,), (1,)), ((), ())),
                preferred_element_type=jnp.float32,
            )
            if bias is not None:
                scores = scores + bias
            row_top = jnp.max(scores, axis=1, keepdims=True)
            if not first:
                old_top = top[h, rows, :]
                row_top = jnp.maximum(row_top, old_top)
            row_exp = jnp.exp2((scores - row_top) * EXP_SCALE)
            row_sum = jnp.sum(row_exp, axis=1, keepdims=True)
            part = jnp.dot(
                row_exp.astype(jnp.bfloat16), value_head, preferred_element_type=jnp.float32
            )
            if not first:
                shrink = jnp.exp2((old_top - row_top) * EXP_SCALE)
                row_sum = row_sum + total[h, rows, :] * shrink
                part = part + acc[h, rows, :] * shrink
            top[h, rows, :] = row_top
            total[h, rows, :] = row_sum
            acc[h, rows, :] = part

    def near_step(h):
        for which in range(2):
            near_copy(h, which).wait_recv()
            if relays:

                @pl.when(is_end)
                def _(which=which):
                    far_copy(h, which).start()

        step(h, near[0, h], near[1, h])

    def first_pass(h, carry):
        query_load(h).wait()
        for which in range(2):
            own_load(h, which).wait()
        step(h, own[0, h], own[1, h], first=True)

        @pl.when(is_end)
        def _():
            near_step(h)

        return carry

    lax.fori_loop(0, heads_here, first_pass, 0)

    def take_blocks(offset, carry):
        block_arrival(offset).wait_recv()
        return carry

    lax.fori_loop(1, owners, take_blocks, 0)

    def second_pass(h, carry):
        cached = [arrived[:, which, :, columns(h)].reshape(-1, HS) for which in range(2)]
        step(h, cached[0], cached[1], bias=bias_row)

        @pl.when(is_mid)
        def _():
            near_step(h)
            for which in range(2):
                far_copy(h, which).wait_recv()
            step(h, far[0, h], far[1, h])

        result[h] = (acc[h] / total[h]).astype(result.dtype)
        result_store(h).start()
        return carry

    lax.fori_loop(0, heads_here, second_pass, 0)

    def finish_blocks(offset, carry):
        block_copy(offset).wait_send()
        return carry

    def finish_near(h, carry):
        result_store(h).wait()
        for which in range(2):
            near_copy(h, which).wait_send()
        return carry

    def finish_far(h, carry):
        for which in range(2):
            far_copy(h, which).wait_send()
        return carry

    lax.fori_loop(1, owners, finish_blocks, 0)
    lax.fori_loop(0, heads_here, finish_near, 0)

    @pl.when(is_end if relays else is_mid)
    def _():
        lax.fori_loop(0, heads_here, finish_far, 0)


def local(queries, keys, values, cache_keys, cache_values, block_list, block_counts):
    tile_count = lax.axis_size("space")
    groups = lax.axis_size("heads")
    tok_rows, col_width = queries.shape
    per_owner, block_rows, full_width = cache_keys.shape
    owners = tile_count * groups
    heads_here = col_width // HS
    scalars = pl.BlockSpec(memory_space=pltpu.SMEM)
    whole = pl.BlockSpec(memory_space=pl.ANY)
    tile_shape = (2, heads_here, tok_rows, HS)
    blocks_shape = (owners, 2, CAP * block_rows, col_width)
    per_head = pltpu.SemaphoreType.DMA((2, heads_here))
    one_each = pltpu.SemaphoreType.DMA((heads_here,))
    per_owner_sem = pltpu.SemaphoreType.DMA((owners,))
    return pl.pallas_call(
        functools.partial(kernel, tile_count, groups),
        out_shape=jax.ShapeDtypeStruct(queries.shape, queries.dtype),
        in_specs=[scalars] * 2 + [whole] * 5,
        out_specs=whole,
        scratch_shapes=[
            pltpu.VMEM(tile_shape[1:], jnp.bfloat16),
            pltpu.VMEM(tile_shape, jnp.bfloat16),
            pltpu.VMEM((2, *cache_keys.shape), jnp.bfloat16),
            pltpu.VMEM(tile_shape[1:], jnp.bfloat16),
            pltpu.VMEM(blocks_shape, jnp.bfloat16),
            pltpu.VMEM(tile_shape, jnp.bfloat16),
            pltpu.VMEM(tile_shape, jnp.bfloat16),
            pltpu.VMEM(blocks_shape, jnp.bfloat16),
            pltpu.VMEM((heads_here, tok_rows, HS), jnp.float32),
            pltpu.VMEM((heads_here, tok_rows, 1), jnp.float32),
            pltpu.VMEM((heads_here, tok_rows, 1), jnp.float32),
            per_head, per_head, per_head, per_head, per_owner_sem, per_owner_sem,
            one_each, per_head, pltpu.SemaphoreType.DMA((2,)), one_each,
        ],
        compiler_params=pltpu.CompilerParams(
            collective_id=0, has_side_effects=True, vmem_limit_bytes=60 * 1024 * 1024
        ),
    )(block_list, block_counts, queries, keys, values, cache_keys, cache_values)


def local_sides(queries, keys, values, cache_keys, cache_values, block_list, block_counts):
    groups = lax.axis_size("heads")
    tok_rows, col_width = queries.shape
    _, block_rows, _ = cache_keys.shape
    heads_here = col_width // HS
    waves = heads_here // 2 if heads_here % 2 == 0 else 1
    side = 2 * groups
    scalars = pl.BlockSpec(memory_space=pltpu.SMEM)
    whole = pl.BlockSpec(memory_space=pl.ANY)
    rows_shape = (heads_here, tok_rows, HS)
    blocks_shape = (heads_here, side, 2, 2, CAP * block_rows, HS)
    rows16 = pltpu.VMEM(rows_shape, jnp.bfloat16)
    logs = pltpu.VMEM((heads_here, 1, tok_rows), jnp.float32)
    per_head = pltpu.SemaphoreType.DMA((2, heads_here))
    one_each = pltpu.SemaphoreType.DMA((heads_here,))
    per_peer = pltpu.SemaphoreType.DMA((waves, side))
    return pl.pallas_call(
        functools.partial(side_kernel, groups, waves),
        out_shape=pltpu.VMEM(queries.shape, queries.dtype),
        in_specs=[scalars] * 2 + [whole] * 5,
        out_specs=pl.BlockSpec(memory_space=pltpu.VMEM),
        scratch_shapes=[
            rows16,
            pltpu.VMEM((2, *rows_shape), jnp.bfloat16),
            rows16, rows16,
            pltpu.VMEM((2, *cache_keys.shape), jnp.bfloat16),
            pltpu.VMEM(blocks_shape, jnp.bfloat16),
            pltpu.VMEM(blocks_shape, jnp.bfloat16),
            pltpu.VMEM(rows_shape, jnp.float32), logs,
            rows16, logs, rows16, logs, rows16, logs,
            one_each, one_each, one_each, one_each, per_head, per_head, per_head, per_head,
            per_peer, per_peer, one_each, per_head, pltpu.SemaphoreType.DMA((2,)),
        ],
        compiler_params=pltpu.CompilerParams(
            collective_id=1, has_side_effects=True, vmem_limit_bytes=60 * 1024 * 1024
        ),
    )(block_list, block_counts, queries, keys, values, cache_keys, cache_values)


def solution(mesh):
    placed = (
        P(("dp", "space"), "heads"),
        P(("dp", "space"), "heads"),
        P(("dp", "space"), "heads"),
        P(("dp", "space", "heads"), None, None),
        P(("dp", "space", "heads"), None, None),
        P("dp", None),
        P("dp"),
    )
    body = local_sides if mesh.shape["space"] == 4 else local
    return jax.shard_map(
        body, mesh=mesh, in_specs=placed, out_specs=P(("dp", "space"), "heads"), check_vma=False
    )
```

```python
import functools

import jax
import jax.numpy as jnp
from jax import lax
from jax.experimental import pallas as pl
from jax.experimental.pallas import tpu as pltpu
from jax.sharding import PartitionSpec as P

HS = 128
CAP = 2
Q_ROWS = 256
END_LAG, MID_LAG = 3, 1
LAST_STEP = 2
EXP_SCALE = HS ** (-0.5) * 1.4426950408889634
MESH = pl.DeviceIdType.MESH


def side_kernel(
    groups, waves, list_ref, count_ref, q_hbm, k_ref, v_ref, cache_k, cache_v, o_ref,
    q_own, own, q_near, q_far, cache, out_blocks, arrived,
    own_part, own_log, sent_part, sent_log, got_part, got_log, far_part, far_log,
    q_send, q_recv, relay_send, relay_recv, part_send, part_recv, far_send, far_recv,
    block_send, block_recv, q_sem, own_sem, cache_sem,
):
    tok_rows, col_width = k_ref.shape
    per_owner, block_rows, _ = cache_k.shape
    listed = list_ref.shape[1]
    heads_here = col_width // HS
    wave_heads = heads_here // waves
    side = 2 * groups
    video = lax.axis_index("dp")
    tile = lax.axis_index("space")
    group = lax.axis_index("heads")
    odd = lax.rem(tile, 2)
    tile_y = tile // 2
    near_tile = tile + 1 - 2 * odd
    far_tile = lax.rem(tile + 2, 4)
    me = tile_y * groups + group
    is_end = jnp.logical_or(tile == 0, tile == 3)
    is_mid = jnp.logical_not(is_end)
    near_device = (video, near_tile, group)
    far_device = (video, far_tile, group)

    def columns(h):
        return pl.ds(pl.multiple_of(h * HS, HS), HS)

    def cache_load(which):
        return pltpu.make_async_copy(
            (cache_k, cache_v)[which], cache.at[which], cache_sem.at[which]
        )

    def query_load(h):
        return pltpu.make_async_copy(q_hbm.at[:, columns(h)], q_own.at[h], q_sem.at[h])

    def own_load(h, which):
        return pltpu.make_async_copy(
            (k_ref, v_ref)[which].at[:, columns(h)], own.at[which, h], own_sem.at[which, h]
        )

    def remote(src, dst, send_sem, recv_sem, device):
        return pltpu.make_async_remote_copy(
            src_ref=src, dst_ref=dst, send_sem=send_sem, recv_sem=recv_sem,
            device_id=device, device_id_type=MESH,
        )

    def query_copy(h):
        return remote(
            q_hbm.at[:, columns(h)], q_near.at[h], q_send.at[h], q_recv.at[h], near_device
        )

    def relay_copy(h):
        return remote(q_near.at[h], q_far.at[h], relay_send.at[h], relay_recv.at[h], far_device)

    def part_copy(h, which):
        src, dst = ((sent_part, got_part), (sent_log, got_log))[which]
        return remote(
            src.at[h], dst.at[h], part_send.at[which, h], part_recv.at[which, h], near_device
        )

    def far_copy(h, which):
        buffer = (far_part, far_log)[which]
        return remote(
            buffer.at[h], buffer.at[h], far_send.at[which, h], far_recv.at[which, h], far_device
        )

    def peer(offset):
        other = lax.rem(me + offset, side)
        return other, (video, odd + 2 * (other // groups), lax.rem(other, groups))

    def wave_part(wave):
        return pl.ds(wave * wave_heads, wave_heads)

    def block_copy(wave, offset):
        other, device = peer(offset)
        return remote(
            out_blocks.at[wave_part(wave), other], arrived.at[wave_part(wave), me],
            block_send.at[wave, offset], block_recv.at[wave, me], device,
        )

    def block_arrival(wave, offset):
        other, device = peer(offset)
        return remote(
            out_blocks.at[wave_part(wave), other], arrived.at[wave_part(wave), other],
            block_send.at[wave, offset], block_recv.at[wave, other], device,
        )

    def start_loads(h, carry):
        query_load(h).start()
        for which in range(2):
            own_load(h, which).start()
        return carry

    for which in range(2):
        cache_load(which).start()

    barrier = pltpu.get_barrier_semaphore()

    def step_of(row, group_at):
        return jnp.where(group_at == 0, row, 1 + jnp.minimum(group_at, LAST_STEP))

    def peer_step(offset):
        other, _ = peer(offset)
        return step_of(other // groups, lax.rem(other, groups))

    step = step_of(tile_y, group)

    def greet(same):
        def one(offset, carry):
            _, device = peer(offset)

            @pl.when((peer_step(offset) == step) == same)
            def _():
                pl.semaphore_signal(barrier, inc=1, device_id=device, device_id_type=MESH)

            return carry

        lax.fori_loop(1, side, one, 0)

    pl.semaphore_signal(barrier, inc=1, device_id=near_device, device_id_type=MESH)
    greet(True)
    lax.fori_loop(0, heads_here, start_loads, 0)
    earlier = 1 + sum((peer_step(offset) <= step).astype(jnp.int32) for offset in range(1, side))
    pl.semaphore_wait(barrier, earlier)

    def start_queries(h, carry):
        query_copy(h).start()
        return carry

    lax.fori_loop(0, heads_here, start_queries, 0)
    greet(False)
    for which in range(2):
        cache_load(which).wait()

    def pack(to_tile, carry):
        def pick(m, state):
            seen, *ids = state
            block = list_ref[to_tile, m]
            owner = block // per_owner
            mine = jnp.logical_and(owner == tile * groups + group, m < count_ref[to_tile])
            ids = [
                jnp.where(jnp.logical_and(mine, seen == slot), lax.rem(block, per_owner), ids[slot])
                for slot in range(CAP)
            ]
            return (seen + mine.astype(jnp.int32), *ids)

        zero = jnp.int32(0)
        _, *ids = lax.fori_loop(0, listed, pick, (zero,) * (CAP + 1))
        crossed = lax.rem(to_tile + odd, 2)
        for which in range(2):
            for slot in range(CAP):
                block = cache[which, ids[slot]]
                for to_group in range(groups):
                    for h in range(heads_here):
                        start = to_group * col_width + h * HS
                        out_blocks[
                            h, to_tile // 2 * groups + to_group, crossed, which,
                            pl.ds(slot * block_rows, block_rows), :
                        ] = block[:, start : start + HS]
        return carry

    lax.fori_loop(0, 4, pack, 0)

    def start_blocks(wave):
        def start(offset, carry):
            block_copy(wave, offset).start()
            return carry

        lax.fori_loop(1, side, start, 0)


    @pl.when(earlier < side)
    def _():
        pl.semaphore_wait(barrier, side - earlier)

    for wave in range(min(waves, 2)):
        start_blocks(wave)

    slots_wide = side * CAP * block_rows
    lane = lax.broadcasted_iota(jnp.int32, (1, slots_wide), 1)
    lane_side = lane // (CAP * block_rows)
    lane_owner = (odd + 2 * (lane_side // groups)) * groups + lax.rem(lane_side, groups)
    lane_slot = lax.rem(lane // block_rows, CAP)

    def bias_of(list_tile):
        def hold(m, held):
            live = m < count_ref[list_tile]
            owner = jnp.where(live, list_ref[list_tile, m] // per_owner, -1)
            return held + (lane_owner == owner).astype(jnp.int32)

        held = lax.fori_loop(0, listed, hold, jnp.zeros((1, slots_wide), jnp.int32))
        return jnp.where(lane_slot < held, 0.0, -jnp.inf).astype(jnp.float32)

    own_bias = bias_of(tile)
    near_bias = bias_of(near_tile)

    def keep(h, carry):
        arrived[h, me] = out_blocks[h, me]
        return carry

    lax.fori_loop(0, heads_here, keep, 0)

    def scores_of(query_rows, key_head):
        return lax.dot_general(
            query_rows, key_head, (((1,), (1,)), ((), ())), preferred_element_type=jnp.float32
        )

    def with_ones(value_head):
        return jnp.concatenate([value_head, jnp.ones(value_head.shape, value_head.dtype)], axis=1)

    def to_row(spread):
        on_diagonal = lax.broadcasted_iota(jnp.int32, (HS, HS), 0) == lax.broadcasted_iota(
            jnp.int32, (HS, HS), 1
        )
        pieces = [
            jnp.sum(jnp.where(on_diagonal, spread[at : at + HS], 0.0), axis=0, keepdims=True)
            for at in range(0, spread.shape[0], HS)
        ]
        return jnp.concatenate(pieces, axis=1)

    def to_column(row):
        return jnp.broadcast_to(row, (HS, row.shape[1])).T

    def attend(queries, h, emit, listed_at=None, bias=None):
        key_head = own[0, h]
        value_head = with_ones(own[1, h])
        if bias is not None:
            cached_key = arrived[h, :, listed_at, 0].reshape(-1, HS)
            cached_value = with_ones(arrived[h, :, listed_at, 1].reshape(-1, HS))
        def scores_at(at):
            query_rows = queries[h, pl.ds(at * Q_ROWS, Q_ROWS), :]
            cached_scores = None if bias is None else scores_of(query_rows, cached_key) + bias
            return scores_of(query_rows, key_head), cached_scores

        steps = tok_rows // Q_ROWS
        ahead = scores_at(0)
        for at in range(steps):
            scores, cached_scores = ahead
            if at + 1 < steps:
                ahead = scores_at(at + 1)
            row_top = jnp.max(scores, axis=1, keepdims=True)
            if bias is not None:
                row_top = jnp.maximum(row_top, jnp.max(cached_scores, axis=1, keepdims=True))
            row_exp = jnp.exp2((scores - row_top) * EXP_SCALE).astype(jnp.bfloat16)
            part = jnp.dot(row_exp, value_head, preferred_element_type=jnp.float32)
            if bias is not None:
                row_exp = jnp.exp2((cached_scores - row_top) * EXP_SCALE).astype(jnp.bfloat16)
                part = part + jnp.dot(row_exp, cached_value, preferred_element_type=jnp.float32)
            total = part[:, HS:]
            rows = pl.ds(at * Q_ROWS, Q_ROWS)
            emit(rows, part[:, :HS] / total, row_top * EXP_SCALE + jnp.log2(total))

    def emit_to(part_ref, log_ref, h):
        def emit(rows, part, log):
            part_ref[h, rows, :] = part.astype(part_ref.dtype)
            log_ref[h, :, rows] = to_row(log)

        return emit

    def emit_joined(h):
        def emit(rows, part, log):
            other = to_column(far_log[h, :, rows])
            log_top = jnp.maximum(log, other)
            weight = jnp.exp2(log - log_top)
            other_weight = jnp.exp2(other - log_top)
            both = weight + other_weight
            joined = (part * weight + far_part[h, rows, :].astype(jnp.float32) * other_weight) / both
            sent_part[h, rows, :] = joined.astype(sent_part.dtype)
            sent_log[h, :, rows] = to_row(log_top + jnp.log2(both))

        return emit

    def wait_own(h):
        for which in range(2):
            own_load(h, which).wait()

    def take_wave(wave):
        def take(offset, carry):
            block_arrival(wave, offset).wait_recv()
            return carry

        lax.fori_loop(1, side, take, 0)

    def near_and_own(h, emit):
        for wave in range(waves):

            @pl.when(h == wave * wave_heads)
            def _(wave=wave):
                take_wave(wave)

        attend(q_near, h, emit, 1, near_bias)
        for which in range(2):
            part_copy(h, which).start()
        query_load(h).wait()
        attend(q_own, h, emit_to(own_part, own_log, h), 0, own_bias)

    def later_waves(at):
        for wave in range(2, waves):

            @pl.when(at == wave_heads * (wave - 1))
            def _(wave=wave):
                start_blocks(wave)

    def end_turn(at, carry):
        later_waves(at)

        @pl.when(at < heads_here)
        def _():
            wait_own(at)
            query_copy(at).wait_recv()
            relay_copy(at).start()

        @pl.when(at >= END_LAG)
        def _():
            h = at - END_LAG
            for which in range(2):
                far_copy(h, which).wait_recv()
            near_and_own(h, emit_joined(h))

        return carry

    def mid_turn(at, carry):
        later_waves(at)

        @pl.when(at < heads_here)
        def _():
            wait_own(at)
            relay_copy(at).wait_recv()
            attend(q_far, at, emit_to(far_part, far_log, at))
            for which in range(2):
                far_copy(at, which).start()

        @pl.when(at >= MID_LAG)
        def _():
            h = at - MID_LAG
            query_copy(h).wait_recv()
            near_and_own(h, emit_to(sent_part, sent_log, h))

        return carry

    @pl.when(is_end)
    def _():
        lax.fori_loop(0, heads_here + END_LAG, end_turn, 0)

    @pl.when(is_mid)
    def _():
        lax.fori_loop(0, heads_here + MID_LAG, mid_turn, 0)

    def join(h, carry):
        for which in range(2):
            part_copy(h, which).wait_recv()
        for at in range(tok_rows // Q_ROWS):
            rows = pl.ds(at * Q_ROWS, Q_ROWS)
            log, other = own_log[h, :, rows], got_log[h, :, rows]
            log_top = jnp.maximum(log, other)
            weight, other_weight = jnp.exp2(log - log_top), jnp.exp2(other - log_top)
            share = to_column(weight / (weight + other_weight))
            got = got_part[h, rows, :].astype(jnp.float32)
            o_ref[rows, columns(h)] = (got + share * (own_part[h, rows, :] - got)).astype(o_ref.dtype)
        return carry

    lax.fori_loop(0, heads_here, join, 0)

    def finish(h, carry):
        query_copy(h).wait_send()
        for which in range(2):
            part_copy(h, which).wait_send()

        @pl.when(is_end)
        def _():
            relay_copy(h).wait_send()

        @pl.when(is_mid)
        def _():
            for which in range(2):
                far_copy(h, which).wait_send()

        return carry

    def finish_blocks(offset, carry):
        for wave in range(waves):
            block_copy(wave, offset).wait_send()
        return carry

    lax.fori_loop(1, side, finish_blocks, 0)
    lax.fori_loop(0, heads_here, finish, 0)


def kernel(
    tiles, groups, list_ref, count_ref, q_hbm, k_ref, v_ref, cache_k, cache_v, o_hbm,
    q_own, own, cache, result, out_blocks, near, far, arrived, acc, top, total,
    near_send, near_recv, far_send, far_recv, block_send, block_recv,
    q_sem, own_sem, cache_sem, result_sem,
):
    owners = tiles * groups
    tok_rows, col_width = k_ref.shape
    per_owner, block_rows, _ = cache_k.shape
    listed = list_ref.shape[1]
    heads_here = col_width // HS
    relays = tiles == 4
    video = lax.axis_index("dp")
    tile = lax.axis_index("space")
    group = lax.axis_index("heads")
    me = tile * groups + group
    odd = lax.rem(tile, 2)
    pair = tile + 1 - 2 * odd
    is_end = jnp.logical_or(tile == 0, tile == tiles - 1)
    is_mid = jnp.logical_not(is_end)
    across = lax.rem(tile + 2, tiles) if relays else tile - 1 + 2 * odd

    def columns(h):
        return pl.ds(pl.multiple_of(h * HS, HS), HS)

    def cache_load(which):
        return pltpu.make_async_copy(
            (cache_k, cache_v)[which], cache.at[which], cache_sem.at[which]
        )

    def query_load(h):
        return pltpu.make_async_copy(q_hbm.at[:, columns(h)], q_own.at[h], q_sem.at[h])

    def own_load(h, which):
        return pltpu.make_async_copy(
            (k_ref, v_ref)[which].at[:, columns(h)], own.at[which, h], own_sem.at[which, h]
        )

    def result_store(h):
        return pltpu.make_async_copy(result.at[h], o_hbm.at[:, columns(h)], result_sem.at[h])

    def start_loads(h, carry):
        query_load(h).start()
        for which in range(2):
            own_load(h, which).start()
        return carry

    for which in range(2):
        cache_load(which).start()
    lax.fori_loop(0, heads_here, start_loads, 0)

    def peer(offset):
        other = lax.rem(me + offset, owners)
        return other, (video, other // groups, lax.rem(other, groups))

    barrier = pltpu.get_barrier_semaphore()

    def announce(offset, carry):
        _, device = peer(offset)
        pl.semaphore_signal(barrier, inc=1, device_id=device, device_id_type=MESH)
        return carry

    lax.fori_loop(1, owners, announce, 0)
    pl.semaphore_wait(barrier, owners - 1)

    def block_copy(offset):
        other, device = peer(offset)
        return pltpu.make_async_remote_copy(
            src_ref=out_blocks.at[other],
            dst_ref=arrived.at[me],
            send_sem=block_send.at[offset],
            recv_sem=block_recv.at[me],
            device_id=device,
            device_id_type=MESH,
        )

    def block_arrival(offset):
        other, device = peer(offset)
        return pltpu.make_async_remote_copy(
            src_ref=out_blocks.at[other],
            dst_ref=arrived.at[other],
            send_sem=block_send.at[offset],
            recv_sem=block_recv.at[other],
            device_id=device,
            device_id_type=MESH,
        )

    def near_copy(h, which):
        source = (k_ref, v_ref)[which]
        return pltpu.make_async_remote_copy(
            src_ref=source.at[:, columns(h)],
            dst_ref=near.at[which, h],
            send_sem=near_send.at[which, h],
            recv_sem=near_recv.at[which, h],
            device_id=(video, pair, group),
            device_id_type=MESH,
        )

    def far_copy(h, which):
        source = near.at[which, h] if relays else (k_ref, v_ref)[which].at[:, columns(h)]
        return pltpu.make_async_remote_copy(
            src_ref=source,
            dst_ref=far.at[which, h],
            send_sem=far_send.at[which, h],
            recv_sem=far_recv.at[which, h],
            device_id=(video, across, group),
            device_id_type=MESH,
        )

    def start_blocks(offset, carry):
        block_copy(offset).start()
        return carry

    def start_near(h, carry):
        for which in range(2):
            near_copy(h, which).start()
        return carry

    def start_far(h, carry):
        for which in range(2):
            far_copy(h, which).start()
        return carry

    lax.fori_loop(0, heads_here // 2, start_near, 0)
    for which in range(2):
        cache_load(which).wait()

    def pack(to_tile, carry):
        def pick(m, state):
            seen, *ids = state
            block = list_ref[to_tile, m]
            mine = jnp.logical_and(block // per_owner == me, m < count_ref[to_tile])
            ids = [
                jnp.where(jnp.logical_and(mine, seen == slot), lax.rem(block, per_owner), ids[slot])
                for slot in range(CAP)
            ]
            return (seen + mine.astype(jnp.int32), *ids)

        zero = jnp.int32(0)
        _, *ids = lax.fori_loop(0, listed, pick, (zero,) * (CAP + 1))
        for which in range(2):
            for slot in range(CAP):
                block = cache[which, ids[slot]]
                for to_group in range(groups):
                    out_blocks[
                        to_tile * groups + to_group, which, pl.ds(slot * block_rows, block_rows), :
                    ] = block[:, to_group * col_width : (to_group + 1) * col_width]
        return carry

    lax.fori_loop(0, tiles, pack, 0)
    lax.fori_loop(1, owners, start_blocks, 0)
    lax.fori_loop(heads_here // 2, heads_here, start_near, 0)
    if not relays:

        @pl.when(is_mid)
        def _():
            lax.fori_loop(0, heads_here, start_far, 0)

    slots_wide = owners * CAP * block_rows
    lane = lax.broadcasted_iota(jnp.int32, (1, slots_wide), 1)
    lane_owner = lane // (CAP * block_rows)
    lane_slot = lax.rem(lane // block_rows, CAP)

    def hold(m, held):
        live = m < count_ref[tile]
        owner = jnp.where(live, list_ref[tile, m] // per_owner, -1)
        return held + (lane_owner == owner).astype(jnp.int32)

    held = lax.fori_loop(0, listed, hold, jnp.zeros((1, slots_wide), jnp.int32))
    bias_row = jnp.where(lane_slot < held, 0.0, -jnp.inf).astype(jnp.float32)

    arrived[me] = out_blocks[me]

    def step(h, key_head, value_head, first=False, bias=None, last=False):
        for at in range(tok_rows // Q_ROWS):
            rows = pl.ds(at * Q_ROWS, Q_ROWS)
            scores = lax.dot_general(
                q_own[h, rows, :], key_head, (((1,), (1,)), ((), ())),
                preferred_element_type=jnp.float32,
            )
            if bias is not None:
                scores = scores + bias
            row_top = jnp.max(scores, axis=1, keepdims=True)
            if not first:
                old_top = top[h, rows, :]
                row_top = jnp.maximum(row_top, old_top)
            row_exp = jnp.exp2((scores - row_top) * EXP_SCALE)
            row_sum = jnp.sum(row_exp, axis=1, keepdims=True)
            part = jnp.dot(
                row_exp.astype(jnp.bfloat16), value_head, preferred_element_type=jnp.float32
            )
            if not first:
                shrink = jnp.exp2((old_top - row_top) * EXP_SCALE)
                row_sum = row_sum + total[h, rows, :] * shrink
                part = part + acc[h, rows, :] * shrink
            top[h, rows, :] = row_top
            total[h, rows, :] = row_sum
            acc[h, rows, :] = part

    def near_step(h):
        for which in range(2):
            near_copy(h, which).wait_recv()
            if relays:

                @pl.when(is_end)
                def _(which=which):
                    far_copy(h, which).start()

        step(h, near[0, h], near[1, h])

    def first_pass(h, carry):
        query_load(h).wait()
        for which in range(2):
            own_load(h, which).wait()
        step(h, own[0, h], own[1, h], first=True)

        @pl.when(is_end)
        def _():
            near_step(h)

        return carry

    lax.fori_loop(0, heads_here, first_pass, 0)

    def take_blocks(offset, carry):
        block_arrival(offset).wait_recv()
        return carry

    lax.fori_loop(1, owners, take_blocks, 0)

    def second_pass(h, carry):
        cached = [arrived[:, which, :, columns(h)].reshape(-1, HS) for which in range(2)]
        step(h, cached[0], cached[1], bias=bias_row)

        @pl.when(is_mid)
        def _():
            near_step(h)
            for which in range(2):
                far_copy(h, which).wait_recv()
            step(h, far[0, h], far[1, h])

        result[h] = (acc[h] / total[h]).astype(result.dtype)
        result_store(h).start()
        return carry

    lax.fori_loop(0, heads_here, second_pass, 0)

    def finish_blocks(offset, carry):
        block_copy(offset).wait_send()
        return carry

    def finish_near(h, carry):
        result_store(h).wait()
        for which in range(2):
            near_copy(h, which).wait_send()
        return carry

    def finish_far(h, carry):
        for which in range(2):
            far_copy(h, which).wait_send()
        return carry

    lax.fori_loop(1, owners, finish_blocks, 0)
    lax.fori_loop(0, heads_here, finish_near, 0)

    @pl.when(is_end if relays else is_mid)
    def _():
        lax.fori_loop(0, heads_here, finish_far, 0)


def local(queries, keys, values, cache_keys, cache_values, block_list, block_counts):
    tile_count = lax.axis_size("space")
    groups = lax.axis_size("heads")
    tok_rows, col_width = queries.shape
    per_owner, block_rows, full_width = cache_keys.shape
    owners = tile_count * groups
    heads_here = col_width // HS
    scalars = pl.BlockSpec(memory_space=pltpu.SMEM)
    whole = pl.BlockSpec(memory_space=pl.ANY)
    tile_shape = (2, heads_here, tok_rows, HS)
    blocks_shape = (owners, 2, CAP * block_rows, col_width)
    per_head = pltpu.SemaphoreType.DMA((2, heads_here))
    one_each = pltpu.SemaphoreType.DMA((heads_here,))
    per_owner_sem = pltpu.SemaphoreType.DMA((owners,))
    return pl.pallas_call(
        functools.partial(kernel, tile_count, groups),
        out_shape=jax.ShapeDtypeStruct(queries.shape, queries.dtype),
        in_specs=[scalars] * 2 + [whole] * 5,
        out_specs=whole,
        scratch_shapes=[
            pltpu.VMEM(tile_shape[1:], jnp.bfloat16),
            pltpu.VMEM(tile_shape, jnp.bfloat16),
            pltpu.VMEM((2, *cache_keys.shape), jnp.bfloat16),
            pltpu.VMEM(tile_shape[1:], jnp.bfloat16),
            pltpu.VMEM(blocks_shape, jnp.bfloat16),
            pltpu.VMEM(tile_shape, jnp.bfloat16),
            pltpu.VMEM(tile_shape, jnp.bfloat16),
            pltpu.VMEM(blocks_shape, jnp.bfloat16),
            pltpu.VMEM((heads_here, tok_rows, HS), jnp.float32),
            pltpu.VMEM((heads_here, tok_rows, 1), jnp.float32),
            pltpu.VMEM((heads_here, tok_rows, 1), jnp.float32),
            per_head, per_head, per_head, per_head, per_owner_sem, per_owner_sem,
            one_each, per_head, pltpu.SemaphoreType.DMA((2,)), one_each,
        ],
        compiler_params=pltpu.CompilerParams(
            collective_id=0, has_side_effects=True, vmem_limit_bytes=60 * 1024 * 1024
        ),
    )(block_list, block_counts, queries, keys, values, cache_keys, cache_values)


def local_sides(queries, keys, values, cache_keys, cache_values, block_list, block_counts):
    groups = lax.axis_size("heads")
    tok_rows, col_width = queries.shape
    _, block_rows, _ = cache_keys.shape
    heads_here = col_width // HS
    waves = heads_here // 2 if heads_here % 2 == 0 else 1
    side = 2 * groups
    scalars = pl.BlockSpec(memory_space=pltpu.SMEM)
    whole = pl.BlockSpec(memory_space=pl.ANY)
    rows_shape = (heads_here, tok_rows, HS)
    blocks_shape = (heads_here, side, 2, 2, CAP * block_rows, HS)
    rows16 = pltpu.VMEM(rows_shape, jnp.bfloat16)
    logs = pltpu.VMEM((heads_here, 1, tok_rows), jnp.float32)
    per_head = pltpu.SemaphoreType.DMA((2, heads_here))
    one_each = pltpu.SemaphoreType.DMA((heads_here,))
    per_peer = pltpu.SemaphoreType.DMA((waves, side))
    return pl.pallas_call(
        functools.partial(side_kernel, groups, waves),
        out_shape=pltpu.VMEM(queries.shape, queries.dtype),
        in_specs=[scalars] * 2 + [whole] * 5,
        out_specs=pl.BlockSpec(memory_space=pltpu.VMEM),
        scratch_shapes=[
            rows16,
            pltpu.VMEM((2, *rows_shape), jnp.bfloat16),
            rows16, rows16,
            pltpu.VMEM((2, *cache_keys.shape), jnp.bfloat16),
            pltpu.VMEM(blocks_shape, jnp.bfloat16),
            pltpu.VMEM(blocks_shape, jnp.bfloat16),
            pltpu.VMEM(rows_shape, jnp.float32), logs,
            rows16, logs, rows16, logs, rows16, logs,
            one_each, one_each, one_each, one_each, per_head, per_head, per_head, per_head,
            per_peer, per_peer, one_each, per_head, pltpu.SemaphoreType.DMA((2,)),
        ],
        compiler_params=pltpu.CompilerParams(
            collective_id=1, has_side_effects=True, vmem_limit_bytes=60 * 1024 * 1024
        ),
    )(block_list, block_counts, queries, keys, values, cache_keys, cache_values)


def solution(mesh):
    placed = (
        P(("dp", "space"), "heads"),
        P(("dp", "space"), "heads"),
        P(("dp", "space"), "heads"),
        P(("dp", "space", "heads"), None, None),
        P(("dp", "space", "heads"), None, None),
        P("dp", None),
        P("dp"),
    )
    body = local_sides if mesh.shape["space"] == 4 else local
    return jax.shard_map(
        body, mesh=mesh, in_specs=placed, out_specs=P(("dp", "space"), "heads"), check_vma=False
    )
```

```python
import functools

import jax
import jax.numpy as jnp
from jax import lax
from jax.experimental import pallas as pl
from jax.experimental.pallas import tpu as pltpu
from jax.sharding import PartitionSpec as P

HS = 128
CAP = 2
Q_ROWS = 256
END_LAG, MID_LAG = 4, 1
LAST_STEP = 2
EXP_SCALE = HS ** (-0.5) * 1.4426950408889634
MESH = pl.DeviceIdType.MESH


def side_kernel(
    groups, waves, list_ref, count_ref, q_hbm, k_ref, v_ref, cache_k, cache_v, o_ref,
    q_own, own, q_near, q_far, cache, out_blocks, arrived,
    own_part, own_log, sent_part, sent_log, got_part, got_log, far_part, far_log,
    q_send, q_recv, relay_send, relay_recv, part_send, part_recv, far_send, far_recv,
    block_send, block_recv, q_sem, own_sem, cache_sem,
):
    tok_rows, col_width = k_ref.shape
    per_owner, block_rows, _ = cache_k.shape
    listed = list_ref.shape[1]
    heads_here = col_width // HS
    wave_heads = heads_here // waves
    side = 2 * groups
    video = lax.axis_index("dp")
    tile = lax.axis_index("space")
    group = lax.axis_index("heads")
    odd = lax.rem(tile, 2)
    tile_y = tile // 2
    near_tile = tile + 1 - 2 * odd
    far_tile = lax.rem(tile + 2, 4)
    me = tile_y * groups + group
    is_end = jnp.logical_or(tile == 0, tile == 3)
    is_mid = jnp.logical_not(is_end)
    near_device = (video, near_tile, group)
    far_device = (video, far_tile, group)

    def columns(h):
        return pl.ds(pl.multiple_of(h * HS, HS), HS)

    def cache_load(which):
        return pltpu.make_async_copy(
            (cache_k, cache_v)[which], cache.at[which], cache_sem.at[which]
        )

    def query_load(h):
        return pltpu.make_async_copy(q_hbm.at[:, columns(h)], q_own.at[h], q_sem.at[h])

    def own_load(h, which):
        return pltpu.make_async_copy(
            (k_ref, v_ref)[which].at[:, columns(h)], own.at[which, h], own_sem.at[which, h]
        )

    def remote(src, dst, send_sem, recv_sem, device):
        return pltpu.make_async_remote_copy(
            src_ref=src, dst_ref=dst, send_sem=send_sem, recv_sem=recv_sem,
            device_id=device, device_id_type=MESH,
        )

    def query_copy(h):
        return remote(
            q_hbm.at[:, columns(h)], q_near.at[h], q_send.at[h], q_recv.at[h], near_device
        )

    def relay_copy(h):
        return remote(q_near.at[h], q_far.at[h], relay_send.at[h], relay_recv.at[h], far_device)

    def part_copy(h, which):
        src, dst = ((sent_part, got_part), (sent_log, got_log))[which]
        return remote(
            src.at[h], dst.at[h], part_send.at[which, h], part_recv.at[which, h], near_device
        )

    def far_copy(h, which):
        buffer = (far_part, far_log)[which]
        return remote(
            buffer.at[h], buffer.at[h], far_send.at[which, h], far_recv.at[which, h], far_device
        )

    def peer(offset):
        other = lax.rem(me + offset, side)
        return other, (video, odd + 2 * (other // groups), lax.rem(other, groups))

    def wave_part(wave):
        return pl.ds(wave * wave_heads, wave_heads)

    def block_copy(wave, offset):
        other, device = peer(offset)
        return remote(
            out_blocks.at[wave_part(wave), other], arrived.at[wave_part(wave), me],
            block_send.at[wave, offset], block_recv.at[wave, me], device,
        )

    def block_arrival(wave, offset):
        other, device = peer(offset)
        return remote(
            out_blocks.at[wave_part(wave), other], arrived.at[wave_part(wave), other],
            block_send.at[wave, offset], block_recv.at[wave, other], device,
        )

    def start_loads(h, carry):
        query_load(h).start()
        for which in range(2):
            own_load(h, which).start()
        return carry

    for which in range(2):
        cache_load(which).start()

    barrier = pltpu.get_barrier_semaphore()

    def step_of(row, group_at):
        return jnp.where(group_at == 0, row, 1 + jnp.minimum(group_at, LAST_STEP))

    def peer_step(offset):
        other, _ = peer(offset)
        return step_of(other // groups, lax.rem(other, groups))

    step = step_of(tile_y, group)

    def greet(same):
        def one(offset, carry):
            _, device = peer(offset)

            @pl.when((peer_step(offset) == step) == same)
            def _():
                pl.semaphore_signal(barrier, inc=1, device_id=device, device_id_type=MESH)

            return carry

        lax.fori_loop(1, side, one, 0)

    pl.semaphore_signal(barrier, inc=1, device_id=near_device, device_id_type=MESH)
    greet(True)
    lax.fori_loop(0, heads_here, start_loads, 0)
    earlier = 1 + sum((peer_step(offset) <= step).astype(jnp.int32) for offset in range(1, side))
    pl.semaphore_wait(barrier, earlier)

    def start_queries(h, carry):
        query_copy(h).start()
        return carry

    lax.fori_loop(0, heads_here, start_queries, 0)
    greet(False)
    for which in range(2):
        cache_load(which).wait()

    def pack(to_tile, carry):
        def pick(m, state):
            seen, *ids = state
            block = list_ref[to_tile, m]
            owner = block // per_owner
            mine = jnp.logical_and(owner == tile * groups + group, m < count_ref[to_tile])
            ids = [
                jnp.where(jnp.logical_and(mine, seen == slot), lax.rem(block, per_owner), ids[slot])
                for slot in range(CAP)
            ]
            return (seen + mine.astype(jnp.int32), *ids)

        zero = jnp.int32(0)
        _, *ids = lax.fori_loop(0, listed, pick, (zero,) * (CAP + 1))
        crossed = lax.rem(to_tile + odd, 2)
        for which in range(2):
            for slot in range(CAP):
                block = cache[which, ids[slot]]
                for to_group in range(groups):
                    for h in range(heads_here):
                        start = to_group * col_width + h * HS
                        out_blocks[
                            h, to_tile // 2 * groups + to_group, crossed, which,
                            pl.ds(slot * block_rows, block_rows), :
                        ] = block[:, start : start + HS]
        return carry

    lax.fori_loop(0, 4, pack, 0)

    def start_blocks(wave):
        def start(offset, carry):
            block_copy(wave, offset).start()
            return carry

        lax.fori_loop(1, side, start, 0)


    @pl.when(earlier < side)
    def _():
        pl.semaphore_wait(barrier, side - earlier)

    for wave in range(min(waves, 2)):
        start_blocks(wave)

    slots_wide = side * CAP * block_rows
    lane = lax.broadcasted_iota(jnp.int32, (1, slots_wide), 1)
    lane_side = lane // (CAP * block_rows)
    lane_owner = (odd + 2 * (lane_side // groups)) * groups + lax.rem(lane_side, groups)
    lane_slot = lax.rem(lane // block_rows, CAP)

    def bias_of(list_tile):
        def hold(m, held):
            live = m < count_ref[list_tile]
            owner = jnp.where(live, list_ref[list_tile, m] // per_owner, -1)
            return held + (lane_owner == owner).astype(jnp.int32)

        held = lax.fori_loop(0, listed, hold, jnp.zeros((1, slots_wide), jnp.int32))
        return jnp.where(lane_slot < held, 0.0, -jnp.inf).astype(jnp.float32)

    own_bias = bias_of(tile)
    near_bias = bias_of(near_tile)

    def keep(h, carry):
        arrived[h, me] = out_blocks[h, me]
        return carry

    lax.fori_loop(0, heads_here, keep, 0)

    def scores_of(query_rows, key_head):
        return lax.dot_general(
            query_rows, key_head, (((1,), (1,)), ((), ())), preferred_element_type=jnp.float32
        )

    def with_ones(value_head):
        return jnp.concatenate([value_head, jnp.ones(value_head.shape, value_head.dtype)], axis=1)

    def to_row(spread):
        on_diagonal = lax.broadcasted_iota(jnp.int32, (HS, HS), 0) == lax.broadcasted_iota(
            jnp.int32, (HS, HS), 1
        )
        pieces = [
            jnp.sum(jnp.where(on_diagonal, spread[at : at + HS], 0.0), axis=0, keepdims=True)
            for at in range(0, spread.shape[0], HS)
        ]
        return jnp.concatenate(pieces, axis=1)

    def to_column(row):
        return jnp.broadcast_to(row, (HS, row.shape[1])).T

    def attend(queries, h, emit, listed_at=None, bias=None):
        key_head = own[0, h]
        value_head = with_ones(own[1, h])
        if bias is not None:
            cached_key = arrived[h, :, listed_at, 0].reshape(-1, HS)
            cached_value = with_ones(arrived[h, :, listed_at, 1].reshape(-1, HS))
        def scores_at(at):
            query_rows = queries[h, pl.ds(at * Q_ROWS, Q_ROWS), :]
            cached_scores = None if bias is None else scores_of(query_rows, cached_key) + bias
            return scores_of(query_rows, key_head), cached_scores

        steps = tok_rows // Q_ROWS
        ahead = scores_at(0)
        for at in range(steps):
            scores, cached_scores = ahead
            if at + 1 < steps:
                ahead = scores_at(at + 1)
            row_top = jnp.max(scores, axis=1, keepdims=True)
            if bias is not None:
                row_top = jnp.maximum(row_top, jnp.max(cached_scores, axis=1, keepdims=True))
            row_exp = jnp.exp2((scores - row_top) * EXP_SCALE).astype(jnp.bfloat16)
            part = jnp.dot(row_exp, value_head, preferred_element_type=jnp.float32)
            if bias is not None:
                row_exp = jnp.exp2((cached_scores - row_top) * EXP_SCALE).astype(jnp.bfloat16)
                part = part + jnp.dot(row_exp, cached_value, preferred_element_type=jnp.float32)
            total = part[:, HS:]
            rows = pl.ds(at * Q_ROWS, Q_ROWS)
            emit(rows, part[:, :HS] / total, row_top * EXP_SCALE + jnp.log2(total))

    def emit_to(part_ref, log_ref, h):
        def emit(rows, part, log):
            part_ref[h, rows, :] = part.astype(part_ref.dtype)
            log_ref[h, :, rows] = to_row(log)

        return emit

    def emit_joined(h):
        def emit(rows, part, log):
            other = to_column(far_log[h, :, rows])
            log_top = jnp.maximum(log, other)
            weight = jnp.exp2(log - log_top)
            other_weight = jnp.exp2(other - log_top)
            both = weight + other_weight
            joined = (part * weight + far_part[h, rows, :].astype(jnp.float32) * other_weight) / both
            sent_part[h, rows, :] = joined.astype(sent_part.dtype)
            sent_log[h, :, rows] = to_row(log_top + jnp.log2(both))

        return emit

    def wait_own(h):
        for which in range(2):
            own_load(h, which).wait()

    def take_wave(wave):
        def take(offset, carry):
            block_arrival(wave, offset).wait_recv()
            return carry

        lax.fori_loop(1, side, take, 0)

    def near_and_own(h, emit):
        for wave in range(waves):

            @pl.when(h == wave * wave_heads)
            def _(wave=wave):
                take_wave(wave)

        attend(q_near, h, emit, 1, near_bias)
        for which in range(2):
            part_copy(h, which).start()
        query_load(h).wait()
        attend(q_own, h, emit_to(own_part, own_log, h), 0, own_bias)

    def later_waves(at):
        for wave in range(2, waves):

            @pl.when(at == wave_heads * (wave - 1))
            def _(wave=wave):
                start_blocks(wave)

    def end_turn(at, carry):
        later_waves(at)

        @pl.when(at < heads_here)
        def _():
            wait_own(at)
            query_copy(at).wait_recv()
            relay_copy(at).start()

        @pl.when(at >= END_LAG)
        def _():
            h = at - END_LAG
            for which in range(2):
                far_copy(h, which).wait_recv()
            near_and_own(h, emit_joined(h))

        return carry

    def mid_turn(at, carry):
        later_waves(at)

        @pl.when(at < heads_here)
        def _():
            wait_own(at)
            relay_copy(at).wait_recv()
            attend(q_far, at, emit_to(far_part, far_log, at))
            for which in range(2):
                far_copy(at, which).start()

        @pl.when(at >= MID_LAG)
        def _():
            h = at - MID_LAG
            query_copy(h).wait_recv()
            near_and_own(h, emit_to(sent_part, sent_log, h))

        return carry

    @pl.when(is_end)
    def _():
        lax.fori_loop(0, heads_here + END_LAG, end_turn, 0)

    @pl.when(is_mid)
    def _():
        lax.fori_loop(0, heads_here + MID_LAG, mid_turn, 0)

    def join(h, carry):
        for which in range(2):
            part_copy(h, which).wait_recv()
        for at in range(tok_rows // Q_ROWS):
            rows = pl.ds(at * Q_ROWS, Q_ROWS)
            log, other = own_log[h, :, rows], got_log[h, :, rows]
            log_top = jnp.maximum(log, other)
            weight, other_weight = jnp.exp2(log - log_top), jnp.exp2(other - log_top)
            share = to_column(weight / (weight + other_weight))
            got = got_part[h, rows, :].astype(jnp.float32)
            o_ref[rows, columns(h)] = (got + share * (own_part[h, rows, :] - got)).astype(o_ref.dtype)
        return carry

    lax.fori_loop(0, heads_here, join, 0)

    def finish(h, carry):
        query_copy(h).wait_send()
        for which in range(2):
            part_copy(h, which).wait_send()

        @pl.when(is_end)
        def _():
            relay_copy(h).wait_send()

        @pl.when(is_mid)
        def _():
            for which in range(2):
                far_copy(h, which).wait_send()

        return carry

    def finish_blocks(offset, carry):
        for wave in range(waves):
            block_copy(wave, offset).wait_send()
        return carry

    lax.fori_loop(1, side, finish_blocks, 0)
    lax.fori_loop(0, heads_here, finish, 0)


def kernel(
    tiles, groups, list_ref, count_ref, q_hbm, k_ref, v_ref, cache_k, cache_v, o_hbm,
    q_own, own, cache, result, out_blocks, near, far, arrived, acc, top, total,
    near_send, near_recv, far_send, far_recv, block_send, block_recv,
    q_sem, own_sem, cache_sem, result_sem,
):
    owners = tiles * groups
    tok_rows, col_width = k_ref.shape
    per_owner, block_rows, _ = cache_k.shape
    listed = list_ref.shape[1]
    heads_here = col_width // HS
    relays = tiles == 4
    video = lax.axis_index("dp")
    tile = lax.axis_index("space")
    group = lax.axis_index("heads")
    me = tile * groups + group
    odd = lax.rem(tile, 2)
    pair = tile + 1 - 2 * odd
    is_end = jnp.logical_or(tile == 0, tile == tiles - 1)
    is_mid = jnp.logical_not(is_end)
    across = lax.rem(tile + 2, tiles) if relays else tile - 1 + 2 * odd

    def columns(h):
        return pl.ds(pl.multiple_of(h * HS, HS), HS)

    def cache_load(which):
        return pltpu.make_async_copy(
            (cache_k, cache_v)[which], cache.at[which], cache_sem.at[which]
        )

    def query_load(h):
        return pltpu.make_async_copy(q_hbm.at[:, columns(h)], q_own.at[h], q_sem.at[h])

    def own_load(h, which):
        return pltpu.make_async_copy(
            (k_ref, v_ref)[which].at[:, columns(h)], own.at[which, h], own_sem.at[which, h]
        )

    def result_store(h):
        return pltpu.make_async_copy(result.at[h], o_hbm.at[:, columns(h)], result_sem.at[h])

    def start_loads(h, carry):
        query_load(h).start()
        for which in range(2):
            own_load(h, which).start()
        return carry

    for which in range(2):
        cache_load(which).start()
    lax.fori_loop(0, heads_here, start_loads, 0)

    def peer(offset):
        other = lax.rem(me + offset, owners)
        return other, (video, other // groups, lax.rem(other, groups))

    barrier = pltpu.get_barrier_semaphore()

    def announce(offset, carry):
        _, device = peer(offset)
        pl.semaphore_signal(barrier, inc=1, device_id=device, device_id_type=MESH)
        return carry

    lax.fori_loop(1, owners, announce, 0)
    pl.semaphore_wait(barrier, owners - 1)

    def block_copy(offset):
        other, device = peer(offset)
        return pltpu.make_async_remote_copy(
            src_ref=out_blocks.at[other],
            dst_ref=arrived.at[me],
            send_sem=block_send.at[offset],
            recv_sem=block_recv.at[me],
            device_id=device,
            device_id_type=MESH,
        )

    def block_arrival(offset):
        other, device = peer(offset)
        return pltpu.make_async_remote_copy(
            src_ref=out_blocks.at[other],
            dst_ref=arrived.at[other],
            send_sem=block_send.at[offset],
            recv_sem=block_recv.at[other],
            device_id=device,
            device_id_type=MESH,
        )

    def near_copy(h, which):
        source = (k_ref, v_ref)[which]
        return pltpu.make_async_remote_copy(
            src_ref=source.at[:, columns(h)],
            dst_ref=near.at[which, h],
            send_sem=near_send.at[which, h],
            recv_sem=near_recv.at[which, h],
            device_id=(video, pair, group),
            device_id_type=MESH,
        )

    def far_copy(h, which):
        source = near.at[which, h] if relays else (k_ref, v_ref)[which].at[:, columns(h)]
        return pltpu.make_async_remote_copy(
            src_ref=source,
            dst_ref=far.at[which, h],
            send_sem=far_send.at[which, h],
            recv_sem=far_recv.at[which, h],
            device_id=(video, across, group),
            device_id_type=MESH,
        )

    def start_blocks(offset, carry):
        block_copy(offset).start()
        return carry

    def start_near(h, carry):
        for which in range(2):
            near_copy(h, which).start()
        return carry

    def start_far(h, carry):
        for which in range(2):
            far_copy(h, which).start()
        return carry

    lax.fori_loop(0, heads_here // 2, start_near, 0)
    for which in range(2):
        cache_load(which).wait()

    def pack(to_tile, carry):
        def pick(m, state):
            seen, *ids = state
            block = list_ref[to_tile, m]
            mine = jnp.logical_and(block // per_owner == me, m < count_ref[to_tile])
            ids = [
                jnp.where(jnp.logical_and(mine, seen == slot), lax.rem(block, per_owner), ids[slot])
                for slot in range(CAP)
            ]
            return (seen + mine.astype(jnp.int32), *ids)

        zero = jnp.int32(0)
        _, *ids = lax.fori_loop(0, listed, pick, (zero,) * (CAP + 1))
        for which in range(2):
            for slot in range(CAP):
                block = cache[which, ids[slot]]
                for to_group in range(groups):
                    out_blocks[
                        to_tile * groups + to_group, which, pl.ds(slot * block_rows, block_rows), :
                    ] = block[:, to_group * col_width : (to_group + 1) * col_width]
        return carry

    lax.fori_loop(0, tiles, pack, 0)
    lax.fori_loop(1, owners, start_blocks, 0)
    lax.fori_loop(heads_here // 2, heads_here, start_near, 0)
    if not relays:

        @pl.when(is_mid)
        def _():
            lax.fori_loop(0, heads_here, start_far, 0)

    slots_wide = owners * CAP * block_rows
    lane = lax.broadcasted_iota(jnp.int32, (1, slots_wide), 1)
    lane_owner = lane // (CAP * block_rows)
    lane_slot = lax.rem(lane // block_rows, CAP)

    def hold(m, held):
        live = m < count_ref[tile]
        owner = jnp.where(live, list_ref[tile, m] // per_owner, -1)
        return held + (lane_owner == owner).astype(jnp.int32)

    held = lax.fori_loop(0, listed, hold, jnp.zeros((1, slots_wide), jnp.int32))
    bias_row = jnp.where(lane_slot < held, 0.0, -jnp.inf).astype(jnp.float32)

    arrived[me] = out_blocks[me]

    def step(h, key_head, value_head, first=False, bias=None, last=False):
        for at in range(tok_rows // Q_ROWS):
            rows = pl.ds(at * Q_ROWS, Q_ROWS)
            scores = lax.dot_general(
                q_own[h, rows, :], key_head, (((1,), (1,)), ((), ())),
                preferred_element_type=jnp.float32,
            )
            if bias is not None:
                scores = scores + bias
            row_top = jnp.max(scores, axis=1, keepdims=True)
            if not first:
                old_top = top[h, rows, :]
                row_top = jnp.maximum(row_top, old_top)
            row_exp = jnp.exp2((scores - row_top) * EXP_SCALE)
            row_sum = jnp.sum(row_exp, axis=1, keepdims=True)
            part = jnp.dot(
                row_exp.astype(jnp.bfloat16), value_head, preferred_element_type=jnp.float32
            )
            if not first:
                shrink = jnp.exp2((old_top - row_top) * EXP_SCALE)
                row_sum = row_sum + total[h, rows, :] * shrink
                part = part + acc[h, rows, :] * shrink
            top[h, rows, :] = row_top
            total[h, rows, :] = row_sum
            acc[h, rows, :] = part

    def near_step(h):
        for which in range(2):
            near_copy(h, which).wait_recv()
            if relays:

                @pl.when(is_end)
                def _(which=which):
                    far_copy(h, which).start()

        step(h, near[0, h], near[1, h])

    def first_pass(h, carry):
        query_load(h).wait()
        for which in range(2):
            own_load(h, which).wait()
        step(h, own[0, h], own[1, h], first=True)

        @pl.when(is_end)
        def _():
            near_step(h)

        return carry

    lax.fori_loop(0, heads_here, first_pass, 0)

    def take_blocks(offset, carry):
        block_arrival(offset).wait_recv()
        return carry

    lax.fori_loop(1, owners, take_blocks, 0)

    def second_pass(h, carry):
        cached = [arrived[:, which, :, columns(h)].reshape(-1, HS) for which in range(2)]
        step(h, cached[0], cached[1], bias=bias_row)

        @pl.when(is_mid)
        def _():
            near_step(h)
            for which in range(2):
                far_copy(h, which).wait_recv()
            step(h, far[0, h], far[1, h])

        result[h] = (acc[h] / total[h]).astype(result.dtype)
        result_store(h).start()
        return carry

    lax.fori_loop(0, heads_here, second_pass, 0)

    def finish_blocks(offset, carry):
        block_copy(offset).wait_send()
        return carry

    def finish_near(h, carry):
        result_store(h).wait()
        for which in range(2):
            near_copy(h, which).wait_send()
        return carry

    def finish_far(h, carry):
        for which in range(2):
            far_copy(h, which).wait_send()
        return carry

    lax.fori_loop(1, owners, finish_blocks, 0)
    lax.fori_loop(0, heads_here, finish_near, 0)

    @pl.when(is_end if relays else is_mid)
    def _():
        lax.fori_loop(0, heads_here, finish_far, 0)


def local(queries, keys, values, cache_keys, cache_values, block_list, block_counts):
    tile_count = lax.axis_size("space")
    groups = lax.axis_size("heads")
    tok_rows, col_width = queries.shape
    per_owner, block_rows, full_width = cache_keys.shape
    owners = tile_count * groups
    heads_here = col_width // HS
    scalars = pl.BlockSpec(memory_space=pltpu.SMEM)
    whole = pl.BlockSpec(memory_space=pl.ANY)
    tile_shape = (2, heads_here, tok_rows, HS)
    blocks_shape = (owners, 2, CAP * block_rows, col_width)
    per_head = pltpu.SemaphoreType.DMA((2, heads_here))
    one_each = pltpu.SemaphoreType.DMA((heads_here,))
    per_owner_sem = pltpu.SemaphoreType.DMA((owners,))
    return pl.pallas_call(
        functools.partial(kernel, tile_count, groups),
        out_shape=jax.ShapeDtypeStruct(queries.shape, queries.dtype),
        in_specs=[scalars] * 2 + [whole] * 5,
        out_specs=whole,
        scratch_shapes=[
            pltpu.VMEM(tile_shape[1:], jnp.bfloat16),
            pltpu.VMEM(tile_shape, jnp.bfloat16),
            pltpu.VMEM((2, *cache_keys.shape), jnp.bfloat16),
            pltpu.VMEM(tile_shape[1:], jnp.bfloat16),
            pltpu.VMEM(blocks_shape, jnp.bfloat16),
            pltpu.VMEM(tile_shape, jnp.bfloat16),
            pltpu.VMEM(tile_shape, jnp.bfloat16),
            pltpu.VMEM(blocks_shape, jnp.bfloat16),
            pltpu.VMEM((heads_here, tok_rows, HS), jnp.float32),
            pltpu.VMEM((heads_here, tok_rows, 1), jnp.float32),
            pltpu.VMEM((heads_here, tok_rows, 1), jnp.float32),
            per_head, per_head, per_head, per_head, per_owner_sem, per_owner_sem,
            one_each, per_head, pltpu.SemaphoreType.DMA((2,)), one_each,
        ],
        compiler_params=pltpu.CompilerParams(
            collective_id=0, has_side_effects=True, vmem_limit_bytes=60 * 1024 * 1024
        ),
    )(block_list, block_counts, queries, keys, values, cache_keys, cache_values)


def local_sides(queries, keys, values, cache_keys, cache_values, block_list, block_counts):
    groups = lax.axis_size("heads")
    tok_rows, col_width = queries.shape
    _, block_rows, _ = cache_keys.shape
    heads_here = col_width // HS
    waves = heads_here // 2 if heads_here % 2 == 0 else 1
    side = 2 * groups
    scalars = pl.BlockSpec(memory_space=pltpu.SMEM)
    whole = pl.BlockSpec(memory_space=pl.ANY)
    rows_shape = (heads_here, tok_rows, HS)
    blocks_shape = (heads_here, side, 2, 2, CAP * block_rows, HS)
    rows16 = pltpu.VMEM(rows_shape, jnp.bfloat16)
    logs = pltpu.VMEM((heads_here, 1, tok_rows), jnp.float32)
    per_head = pltpu.SemaphoreType.DMA((2, heads_here))
    one_each = pltpu.SemaphoreType.DMA((heads_here,))
    per_peer = pltpu.SemaphoreType.DMA((waves, side))
    return pl.pallas_call(
        functools.partial(side_kernel, groups, waves),
        out_shape=pltpu.VMEM(queries.shape, queries.dtype),
        in_specs=[scalars] * 2 + [whole] * 5,
        out_specs=pl.BlockSpec(memory_space=pltpu.VMEM),
        scratch_shapes=[
            rows16,
            pltpu.VMEM((2, *rows_shape), jnp.bfloat16),
            rows16, rows16,
            pltpu.VMEM((2, *cache_keys.shape), jnp.bfloat16),
            pltpu.VMEM(blocks_shape, jnp.bfloat16),
            pltpu.VMEM(blocks_shape, jnp.bfloat16),
            pltpu.VMEM(rows_shape, jnp.float32), logs,
            rows16, logs, rows16, logs, rows16, logs,
            one_each, one_each, one_each, one_each, per_head, per_head, per_head, per_head,
            per_peer, per_peer, one_each, per_head, pltpu.SemaphoreType.DMA((2,)),
        ],
        compiler_params=pltpu.CompilerParams(
            collective_id=1, has_side_effects=True, vmem_limit_bytes=60 * 1024 * 1024
        ),
    )(block_list, block_counts, queries, keys, values, cache_keys, cache_values)


def solution(mesh):
    placed = (
        P(("dp", "space"), "heads"),
        P(("dp", "space"), "heads"),
        P(("dp", "space"), "heads"),
        P(("dp", "space", "heads"), None, None),
        P(("dp", "space", "heads"), None, None),
        P("dp", None),
        P("dp"),
    )
    body = local_sides if mesh.shape["space"] == 4 else local
    return jax.shard_map(
        body, mesh=mesh, in_specs=placed, out_specs=P(("dp", "space"), "heads"), check_vma=False
    )
```
